128 devices in a mesh: ep: 16 (over z, x), fsdp: 8 (over y, core).
Axes of the slice: x: 4, y: 4, z: 4, core: 2. Of those that a mesh axis runs over, the one named last changes fastest.
Arguments:
- tokens: bfloat16 [4, 768, 2048], P(None, 'ep', 'fsdp'), may hold values from -6 to 6
- gate_up_weight: bfloat16 [128, 2048, 1536], P('ep', 'fsdp'), may hold values from -0.125 to 0.125
- down_weight: bfloat16 [128, 2048, 768], P('ep', 'fsdp'), may hold values from -0.21875 to 0.21875
- placement: int32 [160], replicated, may hold values from 0 to 127, as said below
- copy_ids: int32 [4, 768, 8], P(None, 'ep'), may hold values from 0 to 159, all different within a row; in each aligned block of 48 rows (0 to 47, 48 to 95, ..., all dimensions but the last counted through in order) at most 6 rows name the same one
- gate_codes: int32 [4, 768, 8], P(None, 'ep'), may hold values from 4 to 15
Outputs:
- mixed: bfloat16 [4, 768, 2048], P(None, 'ep', 'fsdp')
The draws below stay inside these ranges and needn't reach their ends.
Inputs may be any that keep to these rules, and one draw needn't show every extreme that they name: `placement`: every expert has a copy, and the 10 copies held by one index of ep have experts e with different e // 8. `copy_ids`: the copies in a row differ; within the 48 rows of one index of ep in one step no copy is named by more than 6 rows.
All inputs are finite; a program needn't handle non-finite values.
Results may differ from the reference program's by a relative error of at most 0.023.
Values may be sent and summed in bfloat16 or wider, within the bound.
A program may use at most 128 MiB of HBM per device.

```python
import math
import jax
import jax.numpy as jnp
import numpy as np
from jax import lax

D = 2048
FF = 768
EXP_EP = 8
TOP = 8
STEPS = 4
ROWS_EP = 48
EXPERTS = 128
COPIES = 160
MOST = 6
ROWS = 768
N_EP = 16
N_FSDP = 8


def draw_placement(key, part):
    owner_count = EXPERTS // EXP_EP
    per_owner = COPIES // owner_count
    first, second, third, fourth = jax.random.split(jax.random.fold_in(key, 7), 4)
    owner_order = jax.random.permutation(first, owner_count)
    offset = jax.random.randint(second, (), 0, owner_count)
    local_order = jax.random.permutation(third, EXP_EP)
    extra_local = jax.random.randint(fourth, (owner_count, per_owner), 0, EXP_EP)
    holders = jnp.arange(owner_count)[:, None]
    column = jnp.arange(per_owner)[None, :]
    owners = owner_order[(holders + column + offset) % owner_count]
    local_ids = jnp.where(column < EXP_EP, local_order[jnp.minimum(column, EXP_EP - 1)], extra_local)
    return (owners * EXP_EP + local_ids).reshape(-1).astype(jnp.int32)


def touch_ends(result, stream_key, low, top_value):
    spot = [jax.random.randint(jax.random.fold_in(stream_key, axis), (), 0, length) for axis, length in enumerate(result.shape)]
    main_axis = result.shape.index(max(result.shape))
    neighbour = spot[:main_axis] + [(spot[main_axis] + 1) % result.shape[main_axis]] + spot[main_axis + 1:]
    return result.at[tuple(spot)].set(low).at[tuple(neighbour)].set(top_value)


def block_scale(key, shape, cuts, low, top_value):
    level = 1.0
    for axis_at, parts in cuts:
        draws = jax.random.uniform(jax.random.fold_in(jax.random.fold_in(key, 6), axis_at), (parts,), jnp.float32, low / len(cuts), top_value / len(cuts))
        level = level * jnp.repeat(jnp.exp(draws), shape[axis_at] // parts).reshape((-1,) + (1,) * (len(shape) - 1 - axis_at))
    return level


def routed_block(stream_key, own, number, rows, number_of, top, most, lean):
    order = jax.random.permutation(stream_key, number_of)
    packed, common = load_shares(number_of, rows * top, most, lean, True), load_shares(number_of, rows * top, most, lean, False)
    places = jnp.arange(number_of)

    def named(tallies, rotation):
        used = int((tallies > 0).sum())
        fixed = max(1, used // 4)
        shifted = fixed + (places - fixed + rotation * (used - fixed)) % max(1, number_of - fixed)
        return jnp.zeros((number_of,), jnp.int32).at[order[jnp.where(places < fixed, places, shifted)]].set(jnp.asarray(tallies, jnp.int32))

    tallies = jnp.where(number % 4 == 0, named(packed, number // 4), named(common, number - number // 4 - 1))
    mixed = jax.random.permutation(jax.random.fold_in(own, 3), number_of)
    giver, taker = mixed[0:number_of // 2 * 2:2], mixed[1:number_of // 2 * 2:2]
    margin = jnp.minimum(tallies[giver] - 1, most - tallies[taker]) // 2
    margin = jnp.where((giver == order[0]) | (taker == order[0]) | (tallies[taker] == 0), 0, jnp.maximum(margin, 0))
    shifted = jax.random.randint(jax.random.fold_in(own, 4), (number_of // 2,), 0, 1 << 20) % (margin + 1)
    tallies = tallies.at[giver].add(-shifted).at[taker].add(shifted)
    items = jnp.searchsorted(jnp.cumsum(tallies), jnp.arange(rows * top), side="right").astype(jnp.int32)
    grid = items.reshape(top, rows).T
    grid = grid[jax.random.permutation(jax.random.fold_in(own, 1), rows)]
    rotation = jax.random.randint(jax.random.fold_in(own, 2), (rows, 1), 0, top)
    return jnp.take_along_axis(grid, (jnp.arange(top)[None, :] + rotation) % top, axis=1)


def load_shares(number_of, total, bound, lean, full):
    weights = [(1 << 20) // math.isqrt(standing ** lean) + 1 for standing in range(1, number_of + 1)]
    largest = bound if full else min(bound, max(-(-total // number_of), total * weights[0] // sum(weights)))
    least = 1 if total - largest >= number_of - 1 else 0
    holding, rest = [largest] + [least] * (number_of - 1), total - largest - least * (number_of - 1)
    while rest > 0:
        candidates = [i for i in range(1, number_of) if holding[i] < largest] or [i for i in range(1, number_of) if holding[i] < bound]
        mass, left = sum([weights[i] for i in candidates]), rest
        for i in candidates:
            addition = min(bound - holding[i], max(1, left * weights[i] // mass), rest)
            holding[i] = holding[i] + addition
            rest = rest - addition
    return np.array(holding)


def normal_values(own_key, dims, scale, bound, cuts=(), kind=jnp.bfloat16):
    factor_of = block_scale(own_key, dims, cuts, -0.22, 0.18) if cuts else 1.0
    drawn = jax.random.normal(own_key, dims, jnp.float32) * scale * factor_of
    return jnp.minimum(jnp.maximum(drawn, -bound), bound).astype(kind)


def setup_inputs(seed: int = 0) -> dict:
    key_list = jax.random.split(jax.random.key(seed), 7)
    tokens = normal_values(key_list[0], (STEPS, ROWS, D), 1.0, 6.0, ((1, 16), (2, 8)))
    gate_up_weight = normal_values(key_list[1], (EXPERTS, D, 2 * FF), D ** -0.5, 0.125, ((0, 16), (1, 8)))
    down_weight = normal_values(key_list[2], (EXPERTS, D, FF), FF ** -0.5, 0.21875, ((0, 16), (1, 8)))
    placement = draw_placement(jax.random.fold_in(key_list[6], 71), 0)
    copy_ids_keys = jax.random.split(jax.random.fold_in(key_list[4], 1), STEPS * ROWS // ROWS_EP)
    copy_ids_turns = jax.random.permutation(jax.random.fold_in(key_list[4], 3), STEPS * ROWS // ROWS_EP)
    copy_ids = jax.vmap(lambda own, number: routed_block(jax.random.fold_in(key_list[4], 2), own, number, ROWS_EP, COPIES, TOP, MOST, 2))(copy_ids_keys, copy_ids_turns).reshape((STEPS, ROWS, TOP))
    gate_codes = touch_ends(jax.random.randint(key_list[5], (STEPS, ROWS, TOP), 4, 16), jax.random.fold_in(key_list[5], 1), 4, 15).astype(jnp.int32)
    return {"tokens": tokens, "gate_up_weight": gate_up_weight, "down_weight": down_weight, "placement": placement, "copy_ids": copy_ids, "gate_codes": gate_codes}


def expert_rows(rows, gate_up, down):
    widths = rows.shape[1] // N_FSDP
    blocks = rows.reshape(rows.shape[0], N_FSDP, widths).astype(jnp.float32)
    pieces = gate_up.reshape(N_FSDP, widths, gate_up.shape[1]).astype(jnp.float32)
    partial_value = jnp.einsum("rbd,bdh->rbh", blocks, pieces)
    rounded = lax.optimization_barrier(partial_value.astype(jnp.bfloat16))
    summed = jnp.sum(rounded.astype(jnp.float32), axis=1)
    hidden = (jax.nn.silu(summed[:, :FF]) * summed[:, FF:]).astype(jnp.bfloat16)
    return jnp.dot(hidden, down.T, preferred_element_type=jnp.float32).astype(jnp.bfloat16)


def reference(tokens, gate_up_weight, down_weight, placement, copy_ids, gate_codes):
    capacity = N_EP * MOST
    assigned = ROWS * TOP

    def one_step(inputs):
        rows, chosen, codes = inputs
        flat_ids = chosen.reshape(-1).astype(jnp.int32)
        onehot = (flat_ids[:, None] == jnp.arange(COPIES, dtype=jnp.int32)[None, :]).astype(jnp.int32)
        ranking = jnp.sum(jnp.cumsum(onehot, axis=0) * onehot, axis=1) - 1
        slots = (flat_ids * capacity + ranking).astype(jnp.int32)
        inverse = jnp.full((COPIES * capacity,), assigned, jnp.int32).at[slots].set(jnp.arange(assigned, dtype=jnp.int32))
        valid = inverse < assigned
        source = (jnp.minimum(inverse, assigned - 1) // TOP).astype(jnp.int32)
        gathered = jnp.where(valid[:, None], rows[source], jnp.zeros((), rows.dtype)).reshape(COPIES, capacity, D)

        def per_copy(item):
            block, expert = item
            return expert_rows(block, gate_up_weight[expert], down_weight[expert])

        results = lax.map(per_copy, (gathered, placement))
        values = results.reshape(COPIES * capacity, D)[slots].reshape(ROWS, TOP, D)
        weights = codes.astype(jnp.float32)
        weights = weights / jnp.sum(weights, axis=1, keepdims=True)
        return jnp.sum(values.astype(jnp.float32) * weights[:, :, None], axis=1).astype(jnp.bfloat16)

    return lax.map(one_step, (tokens, copy_ids, gate_codes))
```

```python
import functools

import jax
import jax.numpy as jnp
from jax import lax
from jax.experimental import pallas as pl
from jax.experimental.pallas import tpu as pltpu
from jax.sharding import PartitionSpec as P

CAP = 2304
TILE = 256
LANES = 512
ALIGN = 16
I32, F32, BF16 = jnp.int32, jnp.float32, jnp.bfloat16


def select_rows(pos, val, offs, first, last, base, lane, tile):
    slot = lax.broadcasted_iota(I32, (tile, LANES), 0)

    def one(e, block):
        where = pos[pl.ds(e, 1), pl.ds(lane, LANES)] - base
        value = 1.0 if val is None else val[pl.ds(e, 1), pl.ds(lane, LANES)]
        return jnp.where(where == slot, value, block)

    return lax.fori_loop(first, last, one, jnp.zeros((tile, LANES), F32)).astype(BF16)


def overlap(offs, base, tile, experts):
    first = jnp.int32(0)
    last = jnp.int32(0)
    for e in range(experts):
        first += jnp.where(offs[e + 1] <= base, 1, 0)
        last += jnp.where(offs[e] < base + tile, 1, 0)
    return first, last


def spread(me, base, codes, tokens, weights, part, pos, val, offs, wbuf, sems, xbuf, pbuf, osem):
    experts = weights.shape[0]
    rows = tokens.shape[0]
    loads = [pltpu.make_async_copy(weights.at[e], wbuf.at[e], sems.at[e]) for e in range(experts)]
    for load in loads:
        load.start()
    tri = (
        lax.broadcasted_iota(I32, (256, 256), 0) < lax.broadcasted_iota(I32, (256, 256), 1)
    ).astype(BF16)
    carry = jnp.zeros((experts, 1), F32)
    for c in range(rows // 256):
        span = slice(c * 256, (c + 1) * 256)
        code = codes[:, span]
        local = (code >> 4) - me[0] * experts
        gates = (code & 15).astype(F32)
        total = jnp.concatenate(
            [
                jnp.sum(jnp.where(local == e, gates, 0.0), axis=0, keepdims=True)
                for e in range(experts)
            ],
            axis=0,
        )
        chosen = (total > 0).astype(F32)
        before = jnp.dot(chosen.astype(BF16), tri, preferred_element_type=F32) + carry
        carry = carry + jnp.sum(chosen, axis=1, keepdims=True)
        val[:, span] = total
        pos[:, span] = jnp.where(total > 0, before, -1e6).astype(I32)
    row_of = lax.broadcasted_iota(I32, (experts, 1), 0)
    total = jnp.int32(0)
    starts = jnp.zeros((experts, 1), I32)
    for e in range(experts):
        count = jnp.sum(jnp.where(row_of == e, carry, 0.0)).astype(I32)
        offs[e] = total
        starts = jnp.where(row_of == e, total, starts)
        total += (count + ALIGN - 1) // ALIGN * ALIGN
    offs[experts] = total
    pos[...] += starts - base[0]

    def gather(j, _):
        at = pl.multiple_of(j * TILE, TILE)
        first, last = overlap(offs, at + base[0], TILE, experts)

        def lanes(c, x):
            lane = pl.multiple_of(c * LANES, LANES)
            hot = select_rows(pos, None, offs, first, last, at, lane, TILE)
            return x + jnp.dot(hot, tokens[pl.ds(lane, LANES), :], preferred_element_type=F32)

        x = lax.fori_loop(
            0, rows // LANES, lanes, jnp.zeros((TILE, tokens.shape[1]), F32)
        )
        xbuf[pl.ds(at, TILE), :] = x.astype(BF16)
        return 0

    lax.fori_loop(0, CAP // TILE, gather, 0)
    xbuf[CAP:, :] = jnp.zeros((TILE, tokens.shape[1]), BF16)

    def group(e, _):
        pltpu.make_async_copy(weights.at[e], wbuf.at[e], sems.at[e]).wait()
        low = jnp.clip(offs[e] - base[0], 0, CAP)
        high = jnp.clip(offs[e + 1] - base[0], 0, CAP)

        def tile(i, _):
            at = pl.multiple_of(low + i * TILE, ALIGN)
            pbuf[pl.ds(at, TILE), :] = jnp.dot(
                xbuf[pl.ds(at, TILE), :], wbuf[e], preferred_element_type=F32
            ).astype(BF16)
            return 0

        return lax.fori_loop(0, (high - low + TILE - 1) // TILE, tile, 0)

    lax.fori_loop(0, experts, group, 0)
    end = jnp.clip(offs[experts] - base[0], 0, CAP)

    def clear(i, _):
        at = pl.multiple_of(end + i * ALIGN, ALIGN)
        pbuf[pl.ds(at, ALIGN), :] = jnp.zeros((ALIGN, pbuf.shape[1]), BF16)
        return 0

    lax.fori_loop(0, (CAP - end) // ALIGN, clear, 0)
    out = pltpu.make_async_copy(pbuf.at[pl.ds(0, CAP)], part, osem)
    out.start()
    out.wait()


def call_spread(me, base, codes, tokens, weights):
    experts, depth, width = weights.shape
    rows = tokens.shape[0]
    smem = pl.BlockSpec(memory_space=pltpu.SMEM)
    vmem = pl.BlockSpec(memory_space=pltpu.VMEM)
    hbm = pl.BlockSpec(memory_space=pl.ANY)
    return pl.pallas_call(
        spread,
        out_shape=(
            jax.ShapeDtypeStruct((CAP, width), BF16),
            jax.ShapeDtypeStruct((experts, rows), I32),
            jax.ShapeDtypeStruct((experts, rows), F32),
            jax.ShapeDtypeStruct((16,), I32),
        ),
        in_specs=[smem, smem, vmem, vmem, hbm],
        out_specs=(hbm, vmem, vmem, smem),
        scratch_shapes=[
            pltpu.VMEM(weights.shape, BF16),
            pltpu.SemaphoreType.DMA((experts,)),
            pltpu.VMEM((CAP + TILE, depth), BF16),
            pltpu.VMEM((CAP + TILE, width), BF16),
            pltpu.SemaphoreType.DMA,
        ],
        compiler_params=pltpu.CompilerParams(vmem_limit_bytes=48 << 20),
        name="spread",
    )(me, base, codes, tokens, weights)


def collect(base, offs, pos, val, hidden, weights, out, wbuf, sems, rbuf, acc):
    experts = weights.shape[0]
    rows = pos.shape[1]
    depth = weights.shape[1]
    for e in range(experts):
        pltpu.make_async_copy(weights.at[e], wbuf.at[e], sems.at[e]).start()

    def group(e, _):
        pltpu.make_async_copy(weights.at[e], wbuf.at[e], sems.at[e]).wait()
        low = jnp.clip(offs[e] - base[0], 0, CAP)
        high = jnp.clip(offs[e + 1] - base[0], 0, CAP)

        def tile(i, _):
            at = pl.multiple_of(jnp.minimum(low + i * TILE, CAP - TILE), ALIGN)
            block = lax.dot_general(
                hidden[pl.ds(at, TILE), :],
                wbuf[e],
                (((1,), (1,)), ((), ())),
                preferred_element_type=F32,
            ).astype(BF16)
            inside = lax.broadcasted_iota(I32, (TILE, 1), 0) + at >= low
            rbuf[pl.ds(at, TILE), :] = jnp.where(inside, block, rbuf[pl.ds(at, TILE), :])
            return 0

        return lax.fori_loop(0, (high - low + TILE - 1) // TILE, tile, 0)

    rbuf[...] = jnp.zeros_like(rbuf)
    lax.fori_loop(0, experts, group, 0)
    acc[...] = jnp.zeros_like(acc)

    def combine(j, _):
        at = pl.multiple_of(j * TILE, TILE)
        first, last = overlap(offs, at + base[0], TILE, experts)

        def lanes(c, _):
            lane = pl.multiple_of(c * LANES, LANES)
            hot = select_rows(pos, val, offs, first, last, at, lane, TILE)
            acc[:, pl.ds(lane, LANES)] += lax.dot_general(
                rbuf[pl.ds(at, TILE), :],
                hot,
                (((0,), (0,)), ((), ())),
                preferred_element_type=F32,
            )
            return 0

        return lax.fori_loop(0, rows // LANES, lanes, 0)

    lax.fori_loop(0, CAP // TILE, combine, 0)

    def flip(c, _):
        lane = pl.multiple_of(c * 256, 256)
        out[pl.ds(lane, 256), :] = acc[:, pl.ds(lane, 256)].T.astype(out.dtype)
        return 0

    lax.fori_loop(0, rows // 256, flip, 0)


def call_collect(base, offs, pos, val, hidden, weights):
    experts, depth, width = weights.shape
    rows = pos.shape[1]
    smem = pl.BlockSpec(memory_space=pltpu.SMEM)
    vmem = pl.BlockSpec(memory_space=pltpu.VMEM)
    hbm = pl.BlockSpec(memory_space=pl.ANY)
    return pl.pallas_call(
        collect,
        out_shape=jax.ShapeDtypeStruct((rows, depth), BF16),
        in_specs=[smem, smem, vmem, vmem, vmem, hbm],
        out_specs=vmem,
        scratch_shapes=[
            pltpu.VMEM(weights.shape, BF16),
            pltpu.SemaphoreType.DMA((experts,)),
            pltpu.VMEM((CAP, depth), BF16),
            pltpu.VMEM((depth, rows), F32),
        ],
        compiler_params=pltpu.CompilerParams(vmem_limit_bytes=48 << 20),
        name="collect",
    )(base, offs, pos, val, hidden, weights)


def local(tokens, gate_up_weight, down_weight, placement, copy_ids, gate_codes):
    steps, rows, depth = tokens.shape
    experts, units = gate_up_weight.shape[0], down_weight.shape[2]
    top = copy_ids.shape[2]
    own = lax.axis_index("ep").astype(I32).reshape(1)
    ids = copy_ids.reshape(steps * rows, top).T
    hot = ids[:, :, None] == jnp.arange(placement.shape[0], dtype=I32)
    expert = jnp.sum(jnp.where(hot, placement, 0), axis=2)
    packed = expert * 16 + gate_codes.reshape(steps * rows, top).T
    codes = lax.all_gather(packed, "ep", axis=1, tiled=True)
    everyone = lax.all_gather(tokens.reshape(steps * rows, depth), "ep", axis=0, tiled=True)
    tally = jnp.sum(
        (codes.reshape(-1) >> 4)[None, :] == jnp.arange(experts * lax.axis_size("ep"), dtype=I32)[:, None],
        axis=1,
        dtype=I32,
    )
    most = jnp.max(jnp.sum(((tally + ALIGN - 1) // ALIGN * ALIGN).reshape(-1, experts), axis=1))

    def chunk(at):
        base = (at * CAP).reshape(1)
        part, pos, val, offs = call_spread(own, base, codes, everyone, gate_up_weight)
        summed = lax.psum_scatter(part, "fsdp", scatter_dimension=0, tiled=True).astype(F32)
        hidden = (jax.nn.silu(summed[:, :units]) * summed[:, units:]).astype(BF16)
        hidden = lax.all_gather(hidden, "fsdp", axis=0, tiled=True)
        return call_collect(base, offs, pos, val, hidden, down_weight)

    mixed = chunk(jnp.int32(0))
    _, mixed = lax.while_loop(
        lambda c: c[0] * CAP < most,
        lambda c: (c[0] + 1, (c[1].astype(F32) + chunk(c[0]).astype(F32)).astype(BF16)),
        (jnp.int32(1), mixed),
    )
    mixed = lax.psum_scatter(mixed, "ep", scatter_dimension=0, tiled=True).astype(F32)
    total = jnp.sum(gate_codes, axis=2).astype(F32)
    return (mixed.reshape(steps, rows, depth) / total[:, :, None]).astype(BF16)


def solution(mesh):
    in_specs = (
        P(None, "ep", "fsdp"),
        P("ep", "fsdp", None),
        P("ep", "fsdp", None),
        P(),
        P(None, "ep", None),
        P(None, "ep", None),
    )
    out_specs = P(None, "ep", "fsdp")
    return jax.shard_map(local, mesh=mesh, in_specs=in_specs, out_specs=out_specs, check_vma=False)
```

```python
import functools

import jax
import jax.numpy as jnp
from jax import lax
from jax.experimental import pallas as pl
from jax.experimental.pallas import tpu as pltpu
from jax.sharding import PartitionSpec as P

I32, F32, BF16 = jnp.int32, jnp.float32, jnp.bfloat16
CAP = 2304
TILE = 256
LANES = 512
ALIGN = 16
WAVES = 6
MESH = pl.DeviceIdType.MESH
SIDE = 4
LOW, HIGH = 0, 1


class Post:
    def __init__(self, sends, recvs):
        self.sends, self.recvs, self.made = sends, recvs, {}

    def send(self, key, src, dst, target):
        number = self.made.setdefault(key, len(self.made))
        copy = pltpu.make_async_remote_copy(
            src_ref=src,
            dst_ref=dst,
            send_sem=self.sends.at[number],
            recv_sem=self.recvs.at[number],
            device_id=target,
            device_id_type=MESH,
        )
        copy.start()
        self.made[key] = number
        setattr(self, "copy_%d" % number, copy)

    def arrived(self, key):
        getattr(self, "copy_%d" % self.made[key]).wait_recv()

    def drain(self):
        for number in self.made.values():
            getattr(self, "copy_%d" % number).wait_send()


def greet(targets):
    barrier = pltpu.get_barrier_semaphore()
    for target in targets:
        pl.semaphore_signal(barrier, inc=1, device_id=target, device_id_type=MESH)
    pl.semaphore_wait(barrier, len(targets))


def torus():
    me = lax.axis_index("ep")
    z, x = lax.div(me, SIDE), lax.rem(me, SIDE)

    def at(dz, dx):
        return lax.rem(z + dz, SIDE) * SIDE + lax.rem(x + dx, SIDE)

    return me, z, x, at


def share(codes, tokens, codes_all, tokens_all, keep, csend, crecv, sends, recvs):
    me, z, x, at = torus()
    greet([{"ep": lax.rem(me + d, SIDE * SIDE)} for d in range(1, SIDE * SIDE)])
    rows, depth = tokens.shape
    half = depth // 2
    near = []
    for d in range(1, SIDE * SIDE):
        copy = pltpu.make_async_remote_copy(
            src_ref=codes,
            dst_ref=codes_all.at[me],
            send_sem=csend.at[d],
            recv_sem=crecv.at[d],
            device_id={"ep": lax.rem(me + d, SIDE * SIDE)},
            device_id_type=MESH,
        )
        copy.start()
        near.append(copy)
    post = Post(sends, recvs)
    mine = pltpu.make_async_copy(tokens, tokens_all.at[me], keep.at[0])
    mine.start()
    mine_codes = pltpu.make_async_copy(codes, codes_all.at[me], keep.at[1])
    mine_codes.start()

    def place(side, first, second):
        return at(second, first) if side == 0 else at(first, second)

    def block(side, first, second, part=None):
        span = slice(None) if part is None else pl.ds(part * (rows // 2), rows // 2)
        return tokens_all.at[place(side, first, second), span, pl.ds(side * half, half)]

    def target(side, axis, step):
        first, second = (step, 0) if axis == 1 else (0, step)
        return {"ep": place(side, first, second)}

    for axis in (1, 2):
        for side in (0, 1):
            own = tokens.at[:, pl.ds(side * half, half)]
            for step in (1, 3):
                post.send((side, axis, 0, step), own, block(side, 0, 0), target(side, axis, step))

    def onward(side, first):
        src = block(side, first, 0)
        for step in (1, 3):
            post.send((side, 2, first, step), src, src, target(side, 2, step))

    for step in (1, 3):
        for side in (0, 1):
            post.arrived((side, 1, 0, step))
            part = LOW if step == 1 else HIGH
            src = block(side, 4 - step, 0, part)
            post.send((side, 1, "far", step), src, src, target(side, 1, step))
            onward(side, 4 - step)

    def relay(side, first):
        for step in (1, 3):
            post.arrived((side, 2, first, step))
            part = LOW if step == 1 else HIGH
            src = block(side, first, 4 - step, part)
            post.send((side, 2, first, "far", step), src, src, target(side, 2, step))

    for side in (0, 1):
        relay(side, 0)
    for side in (0, 1):
        for step in (1, 3):
            post.arrived((side, 1, "far", step))
        onward(side, 2)
    for first in (3, 1, 2):
        for side in (0, 1):
            relay(side, first)
    for first in (0, 3, 1, 2):
        for side in (0, 1):
            for step in (1, 3):
                post.arrived((side, 2, first, "far", step))
    for copy in near:
        copy.wait()
    post.drain()
    mine.wait()
    mine_codes.wait()


def call_share(codes, tokens):
    peers = SIDE * SIDE
    vmem = pl.BlockSpec(memory_space=pltpu.VMEM)
    hbm = pl.BlockSpec(memory_space=pl.ANY)
    return pl.pallas_call(
        share,
        out_shape=(
            jax.ShapeDtypeStruct((peers,) + codes.shape, codes.dtype),
            jax.ShapeDtypeStruct((peers,) + tokens.shape, tokens.dtype),
        ),
        in_specs=[vmem, vmem],
        out_specs=(hbm, hbm),
        scratch_shapes=[
            pltpu.SemaphoreType.DMA((2,)),
            pltpu.SemaphoreType.DMA((peers,)),
            pltpu.SemaphoreType.DMA((peers,)),
            pltpu.SemaphoreType.DMA((40,)),
            pltpu.SemaphoreType.DMA((40,)),
        ],
        compiler_params=pltpu.CompilerParams(collective_id=1, has_side_effects=True),
        name="share",
    )(codes, tokens)


def settle(parts, out, big, mid, small, tiny, sends, recvs):
    me, z, x, at = torus()
    greet([{"ep": at(0, 1)}, {"ep": at(0, 3)}, {"ep": at(1, 0)}, {"ep": at(3, 0)}])
    rows, depth = parts.shape[2:]
    half, lot = depth // 2, rows // 2
    post = Post(sends, recvs)
    axis_one = (x, z)
    axis_two = (z, x)

    def wide(side, step, part):
        to = lax.rem(axis_one[side] + step, SIDE)
        spot = (slice(None), to) if side == 0 else (to, slice(None))
        return parts.at[spot + (pl.ds(part * lot, lot), pl.ds(side * half, half))]

    def target(side, stage, step):
        along_x = (side == 0) == (stage == 1)
        return {"ep": at(0, step) if along_x else at(step, 0)}

    def add(a, b):
        return a[...].astype(F32) + b[...].astype(F32)

    def ring(side, stage, source, slots, fill):
        go = functools.partial(target, side, stage)
        yield
        post.send((side, stage, 0), source(2, LOW), slots.at[0], go(1))
        post.send((side, stage, 1), source(2, HIGH), slots.at[1], go(3))
        yield
        post.send((side, stage, 3), source(1, HIGH), slots.at[3], go(1))
        post.send((side, stage, 2), source(3, LOW), slots.at[2], go(3))
        yield
        post.arrived((side, stage, 0))
        fill[0] = add(source(1, LOW), slots.at[0]).astype(BF16)
        post.send((side, stage, 4), fill.at[0], slots.at[4], go(1))
        post.arrived((side, stage, 1))
        fill[1] = add(source(3, HIGH), slots.at[1]).astype(BF16)
        post.send((side, stage, 5), fill.at[1], slots.at[5], go(3))
        yield
        for slot in (2, 3, 4, 5):
            post.arrived((side, stage, slot))
        yield

    def run(stage, sources, slots, fill):
        rings = [ring(side, stage, sources[side], slots.at[side], fill.at[side]) for side in (0, 1)]
        for _ in range(5):
            for one in rings:
                next(one)

    run(1, [functools.partial(wide, side) for side in (0, 1)], big, mid.at[0])
    sums = mid.at[1]
    for side in (0, 1):
        for part in (LOW, HIGH):
            sums[side, part] = (
                wide(side, 0, part)[...].astype(F32)
                + big[side, 2 + part].astype(F32)
                + big[side, 4 + part].astype(F32)
            ).astype(BF16)

    def narrow(side, step, part):
        return sums.at[side, part, lax.rem(axis_two[side] + step, SIDE)]

    run(2, [functools.partial(narrow, side) for side in (0, 1)], small, tiny)
    for side in (0, 1):
        for part in (LOW, HIGH):
            out[pl.ds(part * lot, lot), pl.ds(side * half, half)] = (
                narrow(side, 0, part)[...].astype(F32)
                + small[side, 2 + part].astype(F32)
                + small[side, 4 + part].astype(F32)
            )
    post.drain()


def call_settle(parts):
    rows, depth = parts.shape[2:]
    lot, half = rows // 2, depth // 2
    vmem = pl.BlockSpec(memory_space=pltpu.VMEM)
    return pl.pallas_call(
        settle,
        out_shape=jax.ShapeDtypeStruct((rows, depth), F32),
        in_specs=[vmem],
        out_specs=vmem,
        scratch_shapes=[
            pltpu.VMEM((2, 6, SIDE, lot, half), BF16),
            pltpu.VMEM((2, 2, 2, SIDE, lot, half), BF16),
            pltpu.VMEM((2, 6, lot, half), BF16),
            pltpu.VMEM((2, 2, lot, half), BF16),
            pltpu.SemaphoreType.DMA((24,)),
            pltpu.SemaphoreType.DMA((24,)),
        ],
        compiler_params=pltpu.CompilerParams(collective_id=2, has_side_effects=True),
        name="settle",
    )(parts)


def blend(waves, part, hidden, own, other, far, direct, summed, fill, made, loads, puts, sends, recvs):
    me = lax.axis_index("fsdp")
    y, core = lax.div(me, 2), lax.rem(me, 2)
    rows = part.shape[3]
    units = part.shape[4] // 2
    partner = {"fsdp": y * 2 + 1 - core}
    sides = {step: {"fsdp": lax.rem(y + step, SIDE) * 2 + core} for step in (1, 3)}
    greet([partner, sides[1], sides[3]])
    post = Post(sends, recvs)

    def chip(step):
        return lax.rem(y + step, SIDE)

    for w in range(waves):
        post.send((w, "swap"), part.at[1 - core, w], other.at[w], partner)
        pltpu.make_async_copy(part.at[core, w], own.at[w], loads.at[w]).start()

    columns = (pl.ds(0, units), pl.ds(units, units))

    def mine(w, step, piece):
        return own.at[w, chip(step), :, columns[piece]]

    def fold(w, step):
        at = chip(step)
        own[w, at] = (own[w, at].astype(F32) + other[w, at].astype(F32)).astype(BF16)

    def first(w):
        pltpu.make_async_copy(part.at[core, w], own.at[w], loads.at[w]).wait()
        post.arrived((w, "swap"))
        fold(w, 2)
        post.send((w, "far", LOW), mine(w, 2, LOW), far.at[w, LOW], sides[1])
        post.send((w, "far", HIGH), mine(w, 2, HIGH), far.at[w, HIGH], sides[3])
        fold(w, 1)
        post.send((w, "direct", HIGH), mine(w, 1, HIGH), direct.at[w, HIGH], sides[1])
        fold(w, 3)
        post.send((w, "direct", LOW), mine(w, 3, LOW), direct.at[w, LOW], sides[3])

    def second(w):
        for piece, step in ((LOW, 1), (HIGH, 3)):
            post.arrived((w, "far", piece))
            fill[w, piece] = (
                mine(w, step, piece)[...].astype(F32) + far[w, piece].astype(F32)
            ).astype(BF16)
            post.send((w, "summed", piece), fill.at[w, piece], summed.at[w, piece], sides[step])

    def third(w):
        fold(w, 0)
        both = []
        for piece in (LOW, HIGH):
            post.arrived((w, "direct", piece))
            post.arrived((w, "summed", piece))
            both.append(
                mine(w, 0, piece)[...].astype(F32)
                + direct[w, piece].astype(F32)
                + summed[w, piece].astype(F32)
            )
        gate, up = both
        made[w] = (gate / (1 + jnp.exp(-gate)) * up).astype(BF16)
        goal = hidden.at[core, w, y]
        for step in (1, 3):
            post.send((w, "round", step), made.at[w], goal, sides[step])
        post.send((w, "cross", 0), made.at[w], goal, partner)
        pltpu.make_async_copy(made.at[w], goal, puts.at[w]).start()

    def fourth(w):
        for step in (1, 3):
            post.arrived((w, "round", step))
            block = hidden.at[core, w, chip(4 - step)]
            piece = block.at[pl.ds((step // 2) * (rows // 2), rows // 2)]
            post.send((w, "relay", step), piece, piece, sides[step])
            post.send((w, "cross", step), block, block, partner)

    def fifth(w):
        for step in (1, 3):
            post.arrived((w, "relay", step))
        block = hidden.at[core, w, chip(2)]
        post.send((w, "cross", 2), block, block, partner)

    stages = (first, second, third, fourth, fifth)
    for turn in range(waves + len(stages) - 1):
        for late in reversed(range(len(stages))):
            if 0 <= turn - late < waves:
                stages[late](turn - late)
    for w in range(waves):
        for piece in (0, 1, 3, 2):
            post.arrived((w, "cross", piece))
        pltpu.make_async_copy(made.at[w], hidden.at[core, w, y], puts.at[w]).wait()
    post.drain()


def call_blend(part, waves):
    cap, width = part.shape
    rows, units = cap // (8 * waves), width // 2
    hbm = pl.BlockSpec(memory_space=pl.ANY)
    hidden = pl.pallas_call(
        functools.partial(blend, waves),
        out_shape=jax.ShapeDtypeStruct((2, waves, SIDE, rows, units), BF16),
        in_specs=[hbm],
        out_specs=hbm,
        scratch_shapes=[
            pltpu.VMEM((waves, SIDE, rows, width), BF16),
            pltpu.VMEM((waves, SIDE, rows, width), BF16),
            pltpu.VMEM((waves, 2, rows, units), BF16),
            pltpu.VMEM((waves, 2, rows, units), BF16),
            pltpu.VMEM((waves, 2, rows, units), BF16),
            pltpu.VMEM((waves, 2, rows, units), BF16),
            pltpu.VMEM((waves, rows, units), BF16),
            pltpu.SemaphoreType.DMA((waves,)),
            pltpu.SemaphoreType.DMA((waves,)),
            pltpu.SemaphoreType.DMA((waves * 15,)),
            pltpu.SemaphoreType.DMA((waves * 15,)),
        ],
        compiler_params=pltpu.CompilerParams(
            collective_id=3, has_side_effects=True, vmem_limit_bytes=48 << 20
        ),
        name="blend",
    )(part.reshape(2, waves, SIDE, rows, width))
    return hidden.reshape(cap, units)


def slots_of(e, offs, base):
    low = jnp.clip(offs[e] - base[0], 0, CAP)
    return low, jnp.clip(offs[e + 1] - base[0], 0, CAP)


def mark(e, offs, base, pos, val, hot):
    rows = pos.shape[1]
    low, high = slots_of(e, offs, base)
    slot = lax.broadcasted_iota(I32, (ALIGN, rows), 0)

    def one(i, _):
        at = pl.multiple_of(low + i * ALIGN, ALIGN)
        value = 1.0 if val is None else val[pl.ds(e, 1), :]
        same = pos[pl.ds(e, 1), :] - at == slot
        hot[pl.ds(at, ALIGN), :] = jnp.where(same, value, 0.0).astype(BF16)
        return 0

    lax.fori_loop(0, lax.div(high - low, ALIGN), one, 0)


def blank(ref, low, high):
    def one(i, _):
        at = pl.multiple_of(low + i * ALIGN, ALIGN)
        ref[pl.ds(at, ALIGN), :] = jnp.zeros((ALIGN, ref.shape[1]), ref.dtype)
        return 0

    lax.fori_loop(0, lax.div(high - low, ALIGN), one, 0)


def spread(
    me, base, codes, tokens, weights, part, pos, val, offs, wbuf, sems, hot, xbuf, pbuf, osem
):
    experts = weights.shape[0]
    rows = tokens.shape[0]
    for e in range(experts):
        pltpu.make_async_copy(weights.at[e], wbuf.at[e], sems.at[e]).start()
    tri = (
        lax.broadcasted_iota(I32, (256, 256), 0) < lax.broadcasted_iota(I32, (256, 256), 1)
    ).astype(BF16)
    carry = jnp.zeros((experts, 1), F32)
    for c in range(rows // 256):
        span = slice(c * 256, (c + 1) * 256)
        code = codes[:, span]
        local = (code >> 4) - me[0] * experts
        gates = (code & 15).astype(F32)
        total = jnp.concatenate(
            [
                jnp.sum(jnp.where(local == e, gates, 0.0), axis=0, keepdims=True)
                for e in range(experts)
            ],
            axis=0,
        )
        chosen = (total > 0).astype(F32)
        before = jnp.dot(chosen.astype(BF16), tri, preferred_element_type=F32) + carry
        carry = carry + jnp.sum(chosen, axis=1, keepdims=True)
        val[:, span] = total
        pos[:, span] = jnp.where(total > 0, before, -1e6).astype(I32)
    row_of = lax.broadcasted_iota(I32, (experts, 1), 0)
    total = jnp.int32(0)
    starts = jnp.zeros((experts, 1), I32)
    for e in range(experts):
        count = jnp.sum(jnp.where(row_of == e, carry, 0.0)).astype(I32)
        offs[e] = total
        starts = jnp.where(row_of == e, total, starts)
        total += (count + ALIGN - 1) // ALIGN * ALIGN
    offs[experts] = total
    pos[...] += starts - base[0]
    end = jnp.clip(total - base[0], 0, CAP)
    tiles = lax.div(end + TILE - 1, TILE)

    def marks(e, _):
        mark(e, offs, base, pos, None, hot)
        return 0

    lax.fori_loop(0, experts, marks, 0)
    blank(hot, end, tiles * TILE)

    def gather(j, _):
        at = pl.multiple_of(j * TILE, TILE)
        xbuf[pl.ds(at, TILE), :] = jnp.dot(
            hot[pl.ds(at, TILE), :], tokens[...], preferred_element_type=F32
        ).astype(BF16)
        return 0

    lax.fori_loop(0, tiles, gather, 0)

    def put(j):
        at = pl.multiple_of(j * TILE, TILE)
        return pltpu.make_async_copy(
            pbuf.at[pl.ds(at, TILE)], part.at[pl.ds(at, TILE)], osem.at[j]
        )

    def start(j, _):
        put(j).start()
        return 0

    def group(e, sent):
        pltpu.make_async_copy(weights.at[e], wbuf.at[e], sems.at[e]).wait()
        low, high = slots_of(e, offs, base)

        def tile(i, _):
            at = pl.multiple_of(low + i * TILE, ALIGN)
            pbuf[pl.ds(at, TILE), :] = jnp.dot(
                xbuf[pl.ds(at, TILE), :], wbuf[e], preferred_element_type=F32
            ).astype(BF16)
            return 0

        lax.fori_loop(0, lax.div(high - low + TILE - 1, TILE), tile, 0)
        ready = lax.div(high, TILE)
        lax.fori_loop(sent, ready, start, 0)
        return ready

    sent = lax.fori_loop(0, experts, group, jnp.int32(0))
    blank(pbuf, end, CAP)
    lax.fori_loop(sent, CAP // TILE, start, 0)
    for j in range(CAP // TILE):
        put(j).wait()


def call_spread(me, base, codes, tokens, weights):
    experts, depth, width = weights.shape
    rows = tokens.shape[0]
    smem = pl.BlockSpec(memory_space=pltpu.SMEM)
    vmem = pl.BlockSpec(memory_space=pltpu.VMEM)
    hbm = pl.BlockSpec(memory_space=pl.ANY)
    return pl.pallas_call(
        spread,
        out_shape=(
            jax.ShapeDtypeStruct((CAP, width), BF16),
            jax.ShapeDtypeStruct((experts, rows), I32),
            jax.ShapeDtypeStruct((experts, rows), F32),
            jax.ShapeDtypeStruct((16,), I32),
        ),
        in_specs=[smem, smem, vmem, vmem, hbm],
        out_specs=(hbm, vmem, vmem, smem),
        scratch_shapes=[
            pltpu.VMEM(weights.shape, BF16),
            pltpu.SemaphoreType.DMA((experts,)),
            pltpu.VMEM((CAP, rows), BF16),
            pltpu.VMEM((CAP + TILE, depth), BF16),
            pltpu.VMEM((CAP + TILE, width), BF16),
            pltpu.SemaphoreType.DMA((CAP // TILE,)),
        ],
        compiler_params=pltpu.CompilerParams(vmem_limit_bytes=56 << 20),
        name="spread",
    )(me, base, codes, tokens, weights)


def collect(base, offs, pos, val, hidden, weights, out, wbuf, sems, hbuf, hsem, hot, rbuf, acc):
    experts = weights.shape[0]
    rows = pos.shape[1]
    for e in range(experts):
        pltpu.make_async_copy(weights.at[e], wbuf.at[e], sems.at[e]).start()
    for j in range(CAP // TILE):
        at = slice(j * TILE, (j + 1) * TILE)
        pltpu.make_async_copy(hidden.at[at], hbuf.at[at], hsem.at[j]).start()
    hbuf[CAP:, :] = jnp.zeros((TILE, hbuf.shape[1]), BF16)
    end = jnp.clip(offs[experts] - base[0], 0, CAP)
    tiles = lax.div(end + TILE - 1, TILE)

    def marks(e, _):
        mark(e, offs, base, pos, val, hot)
        return 0

    lax.fori_loop(0, experts, marks, 0)
    blank(hot, end, tiles * TILE)
    for j in range(CAP // TILE):
        at = slice(j * TILE, (j + 1) * TILE)
        pltpu.make_async_copy(hidden.at[at], hbuf.at[at], hsem.at[j]).wait()

    def group(e, _):
        pltpu.make_async_copy(weights.at[e], wbuf.at[e], sems.at[e]).wait()
        low, high = slots_of(e, offs, base)

        def tile(i, _):
            at = pl.multiple_of(low + i * TILE, ALIGN)
            rbuf[pl.ds(at, TILE), :] = lax.dot_general(
                hbuf[pl.ds(at, TILE), :],
                wbuf[e],
                (((1,), (1,)), ((), ())),
                preferred_element_type=F32,
            ).astype(BF16)
            return 0

        return lax.fori_loop(0, lax.div(high - low + TILE - 1, TILE), tile, 0)

    lax.fori_loop(0, experts, group, 0)
    blank(rbuf, end, tiles * TILE)
    acc[...] = jnp.zeros_like(acc)

    def combine(j, _):
        at = pl.multiple_of(j * TILE, TILE)
        turned = rbuf[pl.ds(at, TILE), :].astype(F32).T.astype(BF16)
        for c in range(rows // LANES):
            lane = slice(c * LANES, (c + 1) * LANES)
            acc[:, lane] += jnp.dot(
                turned, hot[pl.ds(at, TILE), lane], preferred_element_type=F32
            )
        return 0

    lax.fori_loop(0, tiles, combine, 0)

    def flip(c, _):
        lane = pl.multiple_of(c * 256, 256)
        out[pl.ds(lane, 256), :] = acc[:, pl.ds(lane, 256)].T.astype(out.dtype)
        return 0

    lax.fori_loop(0, rows // 256, flip, 0)


def call_collect(base, offs, pos, val, hidden, weights):
    experts, depth, width = weights.shape
    rows = pos.shape[1]
    smem = pl.BlockSpec(memory_space=pltpu.SMEM)
    vmem = pl.BlockSpec(memory_space=pltpu.VMEM)
    hbm = pl.BlockSpec(memory_space=pl.ANY)
    return pl.pallas_call(
        collect,
        out_shape=jax.ShapeDtypeStruct((rows, depth), BF16),
        in_specs=[smem, smem, vmem, vmem, hbm, hbm],
        out_specs=vmem,
        scratch_shapes=[
            pltpu.VMEM(weights.shape, BF16),
            pltpu.SemaphoreType.DMA((experts,)),
            pltpu.VMEM((CAP + TILE, width), BF16),
            pltpu.SemaphoreType.DMA((CAP // TILE,)),
            pltpu.VMEM((CAP, rows), BF16),
            pltpu.VMEM((CAP + TILE, depth), BF16),
            pltpu.VMEM((depth, rows), F32),
        ],
        compiler_params=pltpu.CompilerParams(vmem_limit_bytes=56 << 20),
        name="collect",
    )(base, offs, pos, val, hidden, weights)


def local(tokens, gate_up_weight, down_weight, placement, copy_ids, gate_codes):
    steps, rows, depth = tokens.shape
    experts = gate_up_weight.shape[0]
    top = copy_ids.shape[2]
    peers = lax.axis_size("ep")
    own = lax.axis_index("ep").astype(I32).reshape(1)
    ids = copy_ids.reshape(steps * rows, top).T
    same = ids[:, :, None] == jnp.arange(placement.shape[0], dtype=I32)
    expert = jnp.sum(jnp.where(same, placement, 0), axis=2)
    packed = expert * 16 + gate_codes.reshape(steps * rows, top).T
    codes, everyone = call_share(packed, tokens.reshape(steps * rows, depth))
    codes = codes.transpose(1, 0, 2).reshape(top, peers * steps * rows)
    everyone = everyone.reshape(peers * steps * rows, depth)
    tally = jnp.sum(
        (codes.reshape(-1) >> 4)[None, :] == jnp.arange(experts * peers, dtype=I32)[:, None],
        axis=1,
        dtype=I32,
    )
    most = jnp.max(jnp.sum(((tally + ALIGN - 1) // ALIGN * ALIGN).reshape(-1, experts), axis=1))

    def chunk(at):
        base = (at * CAP).reshape(1)
        part, pos, val, offs = call_spread(own, base, codes, everyone, gate_up_weight)
        hidden = call_blend(part, WAVES)
        return call_collect(base, offs, pos, val, hidden, down_weight)

    mixed = chunk(jnp.int32(0))
    _, mixed = lax.while_loop(
        lambda c: c[0] * CAP < most,
        lambda c: (c[0] + 1, (c[1].astype(F32) + chunk(c[0]).astype(F32)).astype(BF16)),
        (jnp.int32(1), mixed),
    )
    mixed = call_settle(mixed.reshape(SIDE, SIDE, steps * rows, depth))
    total = jnp.sum(gate_codes, axis=2).astype(F32)
    return (mixed.reshape(steps, rows, depth) / total[:, :, None]).astype(BF16)


def solution(mesh):
    in_specs = (
        P(None, "ep", "fsdp"),
        P("ep", "fsdp", None),
        P("ep", "fsdp", None),
        P(),
        P(None, "ep", None),
        P(None, "ep", None),
    )
    out_specs = P(None, "ep", "fsdp")
    return jax.shard_map(local, mesh=mesh, in_specs=in_specs, out_specs=out_specs, check_vma=False)
```

```python
import functools

import jax
import jax.numpy as jnp
from jax import lax
from jax.experimental import pallas as pl
from jax.experimental.pallas import tpu as pltpu
from jax.sharding import PartitionSpec as P

I32, F32, BF16 = jnp.int32, jnp.float32, jnp.bfloat16
TILE = 64
LANES = 512
CHOICES = (7, 8, 9, 10)
MESH = pl.DeviceIdType.MESH
SIDE = 4
LOW, HIGH = 0, 1


class Post:
    def __init__(self, sends, recvs):
        self.sends, self.recvs, self.made = sends, recvs, {}

    def send(self, key, src, dst, target):
        number = self.made.setdefault(key, len(self.made))
        copy = pltpu.make_async_remote_copy(
            src_ref=src,
            dst_ref=dst,
            send_sem=self.sends.at[number],
            recv_sem=self.recvs.at[number],
            device_id=target,
            device_id_type=MESH,
        )
        copy.start()
        self.made[key] = number
        setattr(self, "copy_%d" % number, copy)

    def arrived(self, key):
        getattr(self, "copy_%d" % self.made[key]).wait_recv()

    def drain(self):
        for number in self.made.values():
            getattr(self, "copy_%d" % number).wait_send()


def greet(targets):
    barrier = pltpu.get_barrier_semaphore()
    for target in targets:
        pl.semaphore_signal(barrier, inc=1, device_id=target, device_id_type=MESH)
    pl.semaphore_wait(barrier, len(targets))


def torus():
    me = lax.axis_index("ep")
    z, x = lax.div(me, SIDE), lax.rem(me, SIDE)

    def at(dz, dx):
        return lax.rem(z + dz, SIDE) * SIDE + lax.rem(x + dx, SIDE)

    return me, z, x, at


def share(codes, tokens, codes_all, tokens_all, keep, csend, crecv, sends, recvs):
    me, z, x, at = torus()
    greet([{"ep": lax.rem(me + d, SIDE * SIDE)} for d in range(1, SIDE * SIDE)])
    rows, depth = tokens.shape
    half = depth // 2
    near = []
    for d in range(1, SIDE * SIDE):
        copy = pltpu.make_async_remote_copy(
            src_ref=codes,
            dst_ref=codes_all.at[me],
            send_sem=csend.at[d],
            recv_sem=crecv.at[d],
            device_id={"ep": lax.rem(me + d, SIDE * SIDE)},
            device_id_type=MESH,
        )
        copy.start()
        near.append(copy)
    post = Post(sends, recvs)
    mine = pltpu.make_async_copy(tokens, tokens_all.at[me], keep.at[0])
    mine.start()
    mine_codes = pltpu.make_async_copy(codes, codes_all.at[me], keep.at[1])
    mine_codes.start()

    def place(side, first, second):
        return at(second, first) if side == 0 else at(first, second)

    def block(side, first, second, part=None):
        span = slice(None) if part is None else pl.ds(part * (rows // 2), rows // 2)
        return tokens_all.at[place(side, first, second), span, pl.ds(side * half, half)]

    def target(side, axis, step):
        first, second = (step, 0) if axis == 1 else (0, step)
        return {"ep": place(side, first, second)}

    for axis in (1, 2):
        for side in (0, 1):
            own = tokens.at[:, pl.ds(side * half, half)]
            for step in (1, 3):
                post.send((side, axis, 0, step), own, block(side, 0, 0), target(side, axis, step))

    def onward(side, first):
        src = block(side, first, 0)
        for step in (1, 3):
            post.send((side, 2, first, step), src, src, target(side, 2, step))

    for step in (1, 3):
        for side in (0, 1):
            post.arrived((side, 1, 0, step))
            part = LOW if step == 1 else HIGH
            src = block(side, 4 - step, 0, part)
            post.send((side, 1, "far", step), src, src, target(side, 1, step))
            onward(side, 4 - step)

    def relay(side, first):
        for step in (1, 3):
            post.arrived((side, 2, first, step))
            part = LOW if step == 1 else HIGH
            src = block(side, first, 4 - step, part)
            post.send((side, 2, first, "far", step), src, src, target(side, 2, step))

    for side in (0, 1):
        relay(side, 0)
    for side in (0, 1):
        for step in (1, 3):
            post.arrived((side, 1, "far", step))
        onward(side, 2)
    for first in (3, 1, 2):
        for side in (0, 1):
            relay(side, first)
    for first in (0, 3, 1, 2):
        for side in (0, 1):
            for step in (1, 3):
                post.arrived((side, 2, first, "far", step))
    for copy in near:
        copy.wait()
    post.drain()
    mine.wait()
    mine_codes.wait()


def call_share(codes, tokens):
    peers = SIDE * SIDE
    vmem = pl.BlockSpec(memory_space=pltpu.VMEM)
    hbm = pl.BlockSpec(memory_space=pl.ANY)
    return pl.pallas_call(
        share,
        out_shape=(
            jax.ShapeDtypeStruct((peers,) + codes.shape, codes.dtype),
            jax.ShapeDtypeStruct((peers,) + tokens.shape, tokens.dtype),
        ),
        in_specs=[vmem, vmem],
        out_specs=(hbm, hbm),
        scratch_shapes=[
            pltpu.SemaphoreType.DMA((2,)),
            pltpu.SemaphoreType.DMA((peers,)),
            pltpu.SemaphoreType.DMA((peers,)),
            pltpu.SemaphoreType.DMA((40,)),
            pltpu.SemaphoreType.DMA((40,)),
        ],
        compiler_params=pltpu.CompilerParams(collective_id=1, has_side_effects=True),
        name="share",
    )(codes, tokens)


def settle(parts, out, big, mid, small, tiny, sends, recvs):
    me, z, x, at = torus()
    greet([{"ep": at(0, 1)}, {"ep": at(0, 3)}, {"ep": at(1, 0)}, {"ep": at(3, 0)}])
    rows, depth = parts.shape[2:]
    half, lot = depth // 2, rows // 2
    post = Post(sends, recvs)
    axis_one = (x, z)
    axis_two = (z, x)

    def wide(side, step, part):
        to = lax.rem(axis_one[side] + step, SIDE)
        spot = (slice(None), to) if side == 0 else (to, slice(None))
        return parts.at[spot + (pl.ds(part * lot, lot), pl.ds(side * half, half))]

    def target(side, stage, step):
        along_x = (side == 0) == (stage == 1)
        return {"ep": at(0, step) if along_x else at(step, 0)}

    def add(a, b):
        return a[...].astype(F32) + b[...].astype(F32)

    def ring(side, stage, source, slots, fill):
        go = functools.partial(target, side, stage)
        yield
        post.send((side, stage, 0), source(2, LOW), slots.at[0], go(1))
        post.send((side, stage, 1), source(2, HIGH), slots.at[1], go(3))
        yield
        post.send((side, stage, 3), source(1, HIGH), slots.at[3], go(1))
        post.send((side, stage, 2), source(3, LOW), slots.at[2], go(3))
        yield
        post.arrived((side, stage, 0))
        fill[0] = add(source(1, LOW), slots.at[0]).astype(BF16)
        post.send((side, stage, 4), fill.at[0], slots.at[4], go(1))
        post.arrived((side, stage, 1))
        fill[1] = add(source(3, HIGH), slots.at[1]).astype(BF16)
        post.send((side, stage, 5), fill.at[1], slots.at[5], go(3))
        yield
        for slot in (2, 3, 4, 5):
            post.arrived((side, stage, slot))
        yield

    def run(stage, sources, slots, fill):
        rings = [ring(side, stage, sources[side], slots.at[side], fill.at[side]) for side in (0, 1)]
        for _ in range(5):
            for one in rings:
                next(one)

    run(1, [functools.partial(wide, side) for side in (0, 1)], big, mid.at[0])
    sums = mid.at[1]
    for side in (0, 1):
        for part in (LOW, HIGH):
            sums[side, part] = (
                wide(side, 0, part)[...].astype(F32)
                + big[side, 2 + part].astype(F32)
                + big[side, 4 + part].astype(F32)
            ).astype(BF16)

    def narrow(side, step, part):
        return sums.at[side, part, lax.rem(axis_two[side] + step, SIDE)]

    run(2, [functools.partial(narrow, side) for side in (0, 1)], small, tiny)
    for side in (0, 1):
        for part in (LOW, HIGH):
            out[pl.ds(part * lot, lot), pl.ds(side * half, half)] = (
                narrow(side, 0, part)[...].astype(F32)
                + small[side, 2 + part].astype(F32)
                + small[side, 4 + part].astype(F32)
            )
    post.drain()


def call_settle(parts):
    rows, depth = parts.shape[2:]
    lot, half = rows // 2, depth // 2
    vmem = pl.BlockSpec(memory_space=pltpu.VMEM)
    return pl.pallas_call(
        settle,
        out_shape=jax.ShapeDtypeStruct((rows, depth), F32),
        in_specs=[vmem],
        out_specs=vmem,
        scratch_shapes=[
            pltpu.VMEM((2, 6, SIDE, lot, half), BF16),
            pltpu.VMEM((2, 2, 2, SIDE, lot, half), BF16),
            pltpu.VMEM((2, 6, lot, half), BF16),
            pltpu.VMEM((2, 2, lot, half), BF16),
            pltpu.SemaphoreType.DMA((24,)),
            pltpu.SemaphoreType.DMA((24,)),
        ],
        compiler_params=pltpu.CompilerParams(collective_id=2, has_side_effects=True),
        name="settle",
    )(parts)


WAVE = 256
DEPTH = 8
ORDER = (5, 4, 3, 2, 1, 0, 6)
KINDS = (("swap", 0), ("cross", 4), ("cross", 2)) + tuple(
    (name, step)
    for name in ("far", "direct", "summed", "round", "relay", "cross")
    for step in (1, 3)
)


def route(me, base, codes, pos, val, table):
    experts = pos.shape[0]
    peers, _, rows = codes.shape
    code = jnp.concatenate([codes[p] for p in range(peers)], axis=1)
    tri = (
        lax.broadcasted_iota(I32, (256, 256), 0) < lax.broadcasted_iota(I32, (256, 256), 1)
    ).astype(BF16)
    carry = jnp.zeros((experts, 1), F32)
    for c in range(peers * rows // 256):
        span = slice(c * 256, (c + 1) * 256)
        local = (code[:, span] >> 4) - me[0] * experts
        gates = (code[:, span] & 15).astype(F32)
        total = jnp.concatenate(
            [
                jnp.sum(jnp.where(local == e, gates, 0.0), axis=0, keepdims=True)
                for e in range(experts)
            ],
            axis=0,
        )
        chosen = (total > 0).astype(F32)
        before = jnp.dot(chosen.astype(BF16), tri, preferred_element_type=F32) + carry
        carry = carry + jnp.sum(chosen, axis=1, keepdims=True)
        val[:, span] = total
        pos[:, span] = jnp.where(total > 0, before, -1e6).astype(I32)
    sizes = (carry.astype(I32) + TILE - 1) // TILE * TILE
    row_of = lax.broadcasted_iota(I32, (experts, 1), 0)
    starts = jnp.zeros((experts, 1), I32)
    for e in range(experts - 1):
        starts = starts + jnp.where(row_of > e, sizes[e : e + 1, :], 0)
    pos[...] += starts - base[0]
    slot = lax.broadcasted_iota(I32, (experts, 128), 1) * TILE + base[0]
    past = jnp.where(starts + sizes <= slot, 1, 0)
    table[...] = jnp.minimum(jnp.sum(past, axis=0, keepdims=True), experts - 1)


def call_route(me, base, codes, experts):
    peers, _, rows = codes.shape
    smem = pl.BlockSpec(memory_space=pltpu.SMEM)
    vmem = pl.BlockSpec(memory_space=pltpu.VMEM)
    return pl.pallas_call(
        route,
        out_shape=(
            jax.ShapeDtypeStruct((experts, peers * rows), I32),
            jax.ShapeDtypeStruct((experts, peers * rows), F32),
            jax.ShapeDtypeStruct((1, 128), I32),
        ),
        in_specs=[smem, smem, vmem],
        out_specs=(vmem, vmem, vmem),
        name="route",
    )(me, base, codes)


def core(
    waves,
    table,
    pos,
    val,
    tokens,
    gate_up,
    down,
    out,
    wide,
    narrow,
    wsems,
    hot,
    scale,
    picked,
    parts,
    other,
    far,
    direct,
    summed,
    fill,
    hidden,
    turned,
    acc,
    sends,
    recvs,
):
    me = lax.axis_index("fsdp")
    y, core_at = lax.div(me, 2), lax.rem(me, 2)
    experts, units = down.shape[0], down.shape[2]
    rows = WAVE // 8
    side = WAVE // 2
    tiles = WAVE // TILE
    partner = {"fsdp": y * 2 + 1 - core_at}
    sides = {step: {"fsdp": lax.rem(y + step, SIDE) * 2 + core_at} for step in (1, 3)}
    loads = []
    for e in range(experts):
        loads.append(pltpu.make_async_copy(gate_up.at[e], wide.at[e], wsems.at[e]))
    for e in range(experts):
        loads.append(pltpu.make_async_copy(down.at[e], narrow.at[e], wsems.at[experts + e]))
    for load in loads:
        load.start()
    greet([partner, sides[1], sides[3]])
    columns = (pl.ds(0, units), pl.ds(units, units))

    def half(which):
        return pl.ds(pl.multiple_of(which * side, side), side)

    def block(step):
        at = core_at * side + lax.rem(y + step, SIDE) * rows
        return pl.ds(pl.multiple_of(at, rows), rows)

    def mine(w, step, piece):
        return parts.at[w, block(step), columns[piece]]

    def route_of(kind, w):
        name, step = kind
        piece = LOW if (step == 1) == (name != "direct") else HIGH
        if name == "swap":
            return parts.at[w, half(1 - core_at)], other.at[w], partner
        if name == "far":
            return mine(w, 2, piece), far.at[w, piece], sides[step]
        if name == "direct":
            return mine(w, step, piece), direct.at[w, piece], sides[step]
        if name == "summed":
            return fill.at[w, piece], summed.at[w, piece], sides[step]
        if name == "round":
            own = hidden.at[w, block(0)]
            return own, own, sides[step]
        if name == "cross":
            whole = hidden.at[w, block(4 - step)]
            return whole, whole, partner
        at = core_at * side + lax.rem(y + 4 - step, SIDE) * rows + (step // 2) * (rows // 2)
        part = hidden.at[w, pl.ds(pl.multiple_of(at, rows // 2), rows // 2)]
        return part, part, sides[step]

    def copy(name, step, w):
        src, dst, to = route_of((name, step), w)
        k = KINDS.index((name, step))
        return pltpu.make_async_remote_copy(
            src_ref=src,
            dst_ref=dst,
            send_sem=sends.at[w, k],
            recv_sem=recvs.at[w, k],
            device_id=to,
            device_id_type=MESH,
        )

    slot = lax.broadcasted_iota(I32, (TILE, pos.shape[1]), 0)

    def produce(w):
        spot = lax.rem(w, DEPTH)

        def mark(j, _):
            e = table[w * tiles + j]
            at = pl.multiple_of(j * TILE, TILE)
            same = pos[pl.ds(e, 1), :] - (w * WAVE + at) == slot
            hot[spot, pl.ds(at, TILE), :] = jnp.where(same, 1.0, 0.0).astype(BF16)
            scale[spot, pl.ds(at, TILE), :] = jnp.sum(
                jnp.where(same, val[pl.ds(e, 1), :], 0.0), axis=1, keepdims=True
            )
            return 0

        lax.fori_loop(0, tiles, mark, 0)
        picked[...] = jnp.dot(hot[spot], tokens[...], preferred_element_type=F32).astype(BF16)

        @pl.when(w == 0)
        def _():
            for load in loads[:experts]:
                load.wait()

        def tile(which, j, _):
            j = which * (tiles // 2) + j
            e = table[w * tiles + j]
            at = pl.ds(pl.multiple_of(j * TILE, TILE), TILE)
            parts[w, at, :] = jnp.dot(
                picked[at, :], wide[e], preferred_element_type=F32
            ).astype(BF16)
            return 0

        lax.fori_loop(0, tiles // 2, functools.partial(tile, 1 - core_at), 0)
        copy("swap", 0, w).start()
        lax.fori_loop(0, tiles // 2, functools.partial(tile, core_at), 0)

    def fold(w, step):
        at = pl.ds(pl.multiple_of(lax.rem(y + step, SIDE) * rows, rows), rows)
        parts[w, block(step), :] = parts[w, block(step), :] + other[w, at, :]

    def first(w):
        copy("swap", 0, w).wait_recv()
        fold(w, 2)
        copy("far", 1, w).start()
        copy("far", 3, w).start()
        fold(w, 1)
        copy("direct", 1, w).start()
        fold(w, 3)
        copy("direct", 3, w).start()
        fold(w, 0)

    def second(w):
        for piece, step in ((LOW, 1), (HIGH, 3)):
            copy("far", step, w).wait_recv()
            fill[w, piece] = mine(w, step, piece)[...] + far[w, piece]
            copy("summed", step, w).start()

    def third(w):
        both = []
        for piece, step in ((LOW, 1), (HIGH, 3)):
            copy("direct", 4 - step, w).wait_recv()
            copy("summed", step, w).wait_recv()
            both.append(
                mine(w, 0, piece)[...].astype(F32)
                + direct[w, piece].astype(F32)
                + summed[w, piece].astype(F32)
            )
        gate, up = both
        hidden[w, block(0), :] = (gate / (1 + jnp.exp(-gate)) * up).astype(BF16)
        copy("round", 1, w).start()
        copy("round", 3, w).start()
        copy("cross", 4, w).start()

    def fourth(w):
        for step in (1, 3):
            copy("round", step, w).wait_recv()
            copy("relay", step, w).start()
            copy("cross", step, w).start()

    def fifth(w):
        for step in (1, 3):
            copy("relay", step, w).wait_recv()
        copy("cross", 2, w).start()

    def consume(w):
        spot = lax.rem(w, DEPTH)

        @pl.when(w == 0)
        def _():
            for load in loads[experts:]:
                load.wait()

        for step in (4, 1, 3, 2):
            copy("cross", step, w).wait_recv()

        def tile(j, _):
            e = table[w * tiles + j]
            at = pl.ds(pl.multiple_of(j * TILE, TILE), TILE)
            result = lax.dot_general(
                hidden[w, at, :], narrow[e], (((1,), (1,)), ((), ())), preferred_element_type=F32
            )
            turned[at, :] = result * scale[spot, at, :]
            return 0

        lax.fori_loop(0, tiles, tile, 0)
        flat = turned[...].T.astype(BF16)
        for c in range(pos.shape[1] // LANES):
            lane = pl.ds(c * LANES, LANES)
            acc[:, lane] += jnp.dot(flat, hot[spot, :, lane], preferred_element_type=F32)

    acc[...] = jnp.zeros_like(acc)
    stages = (produce, first, second, third, fourth, fifth, consume)

    def turn(t, _):
        for late in ORDER:
            w = t - late

            @pl.when((w >= 0) & (w < waves))
            def _(late=late, w=w):
                stages[late](w)

        return 0

    lax.fori_loop(0, waves + len(stages) - 1, turn, 0)

    def flip(c, _):
        lane = pl.multiple_of(c * 256, 256)
        out[pl.ds(lane, 256), :] = acc[:, pl.ds(lane, 256)].T.astype(out.dtype)
        return 0

    lax.fori_loop(0, out.shape[0] // 256, flip, 0)

    def drain(w, _):
        for name, step in KINDS:
            copy(name, step, w).wait_send()
        return 0

    lax.fori_loop(0, waves, drain, 0)


def call_core(waves, table, pos, val, tokens, gate_up, down):
    experts, depth, width = gate_up.shape
    rows, units = WAVE // 8, width // 2
    total = tokens.shape[0]
    smem = pl.BlockSpec(memory_space=pltpu.SMEM)
    vmem = pl.BlockSpec(memory_space=pltpu.VMEM)
    hbm = pl.BlockSpec(memory_space=pl.ANY)
    piece = pltpu.VMEM((waves, 2, rows, units), BF16)
    return pl.pallas_call(
        functools.partial(core, waves),
        out_shape=jax.ShapeDtypeStruct((total, depth), BF16),
        in_specs=[smem, vmem, vmem, vmem, hbm, hbm],
        out_specs=vmem,
        scratch_shapes=[
            pltpu.VMEM(gate_up.shape, BF16),
            pltpu.VMEM(down.shape, BF16),
            pltpu.SemaphoreType.DMA((2 * experts,)),
            pltpu.VMEM((DEPTH, WAVE, total), BF16),
            pltpu.VMEM((DEPTH, WAVE, 1), F32),
            pltpu.VMEM((WAVE, depth), BF16),
            pltpu.VMEM((waves, WAVE, width), BF16),
            pltpu.VMEM((waves, WAVE // 2, width), BF16),
            piece,
            piece,
            piece,
            piece,
            pltpu.VMEM((waves, WAVE, units), BF16),
            pltpu.VMEM((WAVE, depth), F32),
            pltpu.VMEM((depth, total), F32),
            pltpu.SemaphoreType.DMA((waves, len(KINDS))),
            pltpu.SemaphoreType.DMA((waves, len(KINDS))),
        ],
        compiler_params=pltpu.CompilerParams(
            collective_id=waves, has_side_effects=True, vmem_limit_bytes=62 << 20
        ),
        name="core%d" % waves,
    )(table, pos, val, tokens, gate_up, down)


def local(tokens, gate_up_weight, down_weight, placement, copy_ids, gate_codes):
    steps, rows, depth = tokens.shape
    experts = gate_up_weight.shape[0]
    top = copy_ids.shape[2]
    peers = lax.axis_size("ep")
    own = lax.axis_index("ep").astype(I32).reshape(1)
    ids = copy_ids.reshape(steps * rows, top).T
    same = ids[:, :, None] == jnp.arange(placement.shape[0], dtype=I32)
    expert = jnp.sum(jnp.where(same, placement, 0), axis=2)
    packed = expert * 16 + gate_codes.reshape(steps * rows, top).T
    codes, everyone = call_share(packed, tokens.reshape(steps * rows, depth))
    everyone = everyone.reshape(peers * steps * rows, depth)
    tally = jnp.sum(
        (codes >> 4)[None] == jnp.arange(experts * peers, dtype=I32)[:, None, None, None],
        axis=(1, 2, 3),
        dtype=I32,
    )
    most = jnp.max(jnp.sum(((tally + TILE - 1) // TILE * TILE).reshape(-1, experts), axis=1))

    def chunk(base, waves):
        pos, val, table = call_route(own, base.reshape(1), codes, experts)
        return call_core(waves, table.reshape(-1), pos, val, everyone, gate_up_weight, down_weight)

    pos, val, table = call_route(own, jnp.zeros((1,), I32), codes, experts)
    branches = [functools.partial(call_core, waves) for waves in CHOICES]
    pick = jnp.int32(0)
    for waves in CHOICES[:-1]:
        pick += (most > waves * WAVE).astype(I32)
    mixed = lax.switch(
        pick, branches, table.reshape(-1), pos, val, everyone, gate_up_weight, down_weight
    )
    span = CHOICES[-1] * WAVE
    _, mixed = lax.while_loop(
        lambda c: c[0] * span < most,
        lambda c: (
            c[0] + 1,
            (c[1].astype(F32) + chunk(c[0] * span, CHOICES[-1]).astype(F32)).astype(BF16),
        ),
        (jnp.int32(1), mixed),
    )
    mixed = call_settle(mixed.reshape(SIDE, SIDE, steps * rows, depth))
    total = jnp.sum(gate_codes, axis=2).astype(F32)
    return (mixed.reshape(steps, rows, depth) / total[:, :, None]).astype(BF16)


def solution(mesh):
    in_specs = (
        P(None, "ep", "fsdp"),
        P("ep", "fsdp", None),
        P("ep", "fsdp", None),
        P(),
        P(None, "ep", None),
        P(None, "ep", None),
    )
    out_specs = P(None, "ep", "fsdp")
    return jax.shard_map(local, mesh=mesh, in_specs=in_specs, out_specs=out_specs, check_vma=False)
```

```python
import functools

import jax
import jax.numpy as jnp
from jax import lax
from jax.experimental import pallas as pl
from jax.experimental.pallas import tpu as pltpu
from jax.sharding import PartitionSpec as P

I32, F32, BF16 = jnp.int32, jnp.float32, jnp.bfloat16
TILE = 64
LANES = 512
CHOICES = (7, 8, 9, 10)
MESH = pl.DeviceIdType.MESH
SIDE = 4
LOW, HIGH = 0, 1


class Post:
    def __init__(self, sends, recvs):
        self.sends, self.recvs, self.made = sends, recvs, {}

    def send(self, key, src, dst, target):
        number = self.made.setdefault(key, len(self.made))
        copy = pltpu.make_async_remote_copy(
            src_ref=src,
            dst_ref=dst,
            send_sem=self.sends.at[number],
            recv_sem=self.recvs.at[number],
            device_id=target,
            device_id_type=MESH,
        )
        copy.start()
        self.made[key] = number
        setattr(self, "copy_%d" % number, copy)

    def arrived(self, key):
        getattr(self, "copy_%d" % self.made[key]).wait_recv()

    def drain(self):
        for number in self.made.values():
            getattr(self, "copy_%d" % number).wait_send()


def greet(targets):
    barrier = pltpu.get_barrier_semaphore()
    for target in targets:
        pl.semaphore_signal(barrier, inc=1, device_id=target, device_id_type=MESH)
    pl.semaphore_wait(barrier, len(targets))


def torus():
    me = lax.axis_index("ep")
    z, x = lax.div(me, SIDE), lax.rem(me, SIDE)

    def at(dz, dx):
        return lax.rem(z + dz, SIDE) * SIDE + lax.rem(x + dx, SIDE)

    return me, z, x, at


def share(raw, placement, tokens, codes_all, tokens_all, codes, keep, sends, recvs):
    me, z, x, at = torus()
    barrier = pltpu.get_barrier_semaphore()
    peers = [(0, step) for step in (1, 2, 3)] + [(step, 0) for step in (1, 2, 3)]
    for dz, dx in peers:
        pl.semaphore_signal(barrier, inc=1, device_id={"ep": at(dz, dx)}, device_id_type=MESH)
    copies = raw[...] >> 4

    def look(i, found):
        return jnp.where(copies == i, placement[i], found)

    found = lax.fori_loop(0, placement.shape[0], look, jnp.zeros_like(copies), unroll=8)
    codes[...] = found * 16 + (raw[...] & 15)
    pl.semaphore_wait(barrier, len(peers))
    rows, depth = tokens.shape
    half = depth // 2
    post = Post(sends, recvs)
    mine_codes = pltpu.make_async_copy(codes, codes_all.at[z, x], keep.at[1])
    mine_codes.start()
    for step in (1, 3, 2):
        post.send(("codes", 1, step), codes, codes_all.at[z, x], {"ep": at(0, step)})

    def place(side, first, second):
        return at(second, first) if side == 0 else at(first, second)

    def block(side, first, second, part=None):
        span = slice(None) if part is None else pl.ds(part * (rows // 2), rows // 2)
        return tokens_all.at[place(side, first, second), span, pl.ds(side * half, half)]

    def target(side, axis, step):
        first, second = (step, 0) if axis == 1 else (0, step)
        return {"ep": place(side, first, second)}

    for axis, steps in ((1, (2, 1, 3)), (2, (1, 3))):
        for side in (0, 1):
            own = tokens.at[:, pl.ds(side * half, half)]
            for step in steps:
                post.send((side, axis, 0, step), own, block(side, 0, 0), target(side, axis, step))
    mine = pltpu.make_async_copy(tokens, tokens_all.at[me], keep.at[0])
    mine.start()

    def onward(side, first, steps):
        src = block(side, first, 0)
        for step in steps:
            post.send((side, 2, first, step), src, src, target(side, 2, step))

    def relay(side, first):
        for step in (1, 3):
            post.arrived((side, 2, first, step))
            part = LOW if step == 1 else HIGH
            src = block(side, first, 4 - step, part)
            post.send((side, 2, first, "far", step), src, src, target(side, 2, step))

    for step in (1, 3, 2):
        post.arrived(("codes", 1, step))
    mine_codes.wait()
    for step in (1, 3, 2):
        post.send(("codes", 2, step), codes_all.at[z], codes_all.at[z], {"ep": at(step, 0)})
    for step in (1, 3):
        for side in (0, 1):
            post.arrived((side, 1, 0, step))
            onward(side, 4 - step, (1, 3))
    for side in (0, 1):
        post.arrived((side, 1, 0, 2))
        onward(side, 2, (2, 1, 3))
    for first in (0, 3, 1):
        for side in (0, 1):
            relay(side, first)
    for first in (0, 3, 1):
        for side in (0, 1):
            for step in (1, 3):
                post.arrived((side, 2, first, "far", step))
    for side in (0, 1):
        for step in (1, 3, 2):
            post.arrived((side, 2, 2, step))
    for step in (1, 3, 2):
        post.arrived(("codes", 2, step))
    post.drain()
    mine.wait()


def call_share(raw, placement, tokens):
    vmem = pl.BlockSpec(memory_space=pltpu.VMEM)
    smem = pl.BlockSpec(memory_space=pltpu.SMEM)
    hbm = pl.BlockSpec(memory_space=pl.ANY)
    return pl.pallas_call(
        share,
        out_shape=(
            jax.ShapeDtypeStruct((SIDE, SIDE) + raw.shape, raw.dtype),
            jax.ShapeDtypeStruct((SIDE * SIDE,) + tokens.shape, tokens.dtype),
        ),
        in_specs=[vmem, smem, vmem],
        out_specs=(hbm, hbm),
        scratch_shapes=[
            pltpu.VMEM(raw.shape, raw.dtype),
            pltpu.SemaphoreType.DMA((2,)),
            pltpu.SemaphoreType.DMA((42,)),
            pltpu.SemaphoreType.DMA((42,)),
        ],
        compiler_params=pltpu.CompilerParams(collective_id=1, has_side_effects=True),
        name="share",
    )(raw, placement, tokens)


def settle(parts, out, big, fills, sums, small, sends, recvs):
    me, z, x, at = torus()
    greet([{"ep": at(0, step)} for step in (1, 2, 3)] + [{"ep": at(step, 0)} for step in (1, 2, 3)])
    rows, depth = parts.shape[2:]
    half, lot = depth // 2, rows // 2
    post = Post(sends, recvs)
    axis_one = (x, z)
    axis_two = (z, x)

    def wide(side, step, part):
        to = lax.rem(axis_one[side] + step, SIDE)
        spot = (slice(None), to) if side == 0 else (to, slice(None))
        return parts.at[spot + (pl.ds(part * lot, lot), pl.ds(side * half, half))]

    def target(side, stage, step):
        along_x = (side == 0) == (stage == 1)
        return {"ep": at(0, step) if along_x else at(step, 0)}

    for side in (0, 1):
        post.send((side, 0), wide(side, 2, LOW), big.at[side, 0], target(side, 1, 1))
        post.send((side, 1), wide(side, 2, HIGH), big.at[side, 1], target(side, 1, 3))
    for side in (0, 1):
        post.send((side, 3), wide(side, 1, HIGH), big.at[side, 3], target(side, 1, 1))
        post.send((side, 2), wide(side, 3, LOW), big.at[side, 2], target(side, 1, 3))
    for side in (0, 1):
        for part, step in ((LOW, 1), (HIGH, 3)):
            post.arrived((side, part))
            fills[side, part] = wide(side, step, part)[...] + big[side, part]
            post.send((side, 4 + part), fills.at[side, part], big.at[side, 4 + part], target(side, 1, step))
    for side in (0, 1):
        for part in (HIGH, LOW):
            post.arrived((side, 2 + part))
            post.arrived((side, 4 + part))
            sums[side, :, pl.ds(part * lot, lot), :] = (
                wide(side, 0, part)[...].astype(F32)
                + big[side, 2 + part].astype(F32)
                + big[side, 4 + part].astype(F32)
            ).astype(BF16)
        for step in (2, 1, 3):
            to = lax.rem(axis_two[side] + step, SIDE)
            post.send((side, "two", step), sums.at[side, to], small.at[side, step - 1], target(side, 2, step))
    for side in (0, 1):
        for step in (1, 3, 2):
            post.arrived((side, "two", step))
        out[:, pl.ds(side * half, half)] = (
            sums[side, axis_two[side]].astype(F32)
            + small[side, 0].astype(F32)
            + small[side, 1].astype(F32)
            + small[side, 2].astype(F32)
        )
    post.drain()


def call_settle(parts):
    rows, depth = parts.shape[2:]
    lot, half = rows // 2, depth // 2
    vmem = pl.BlockSpec(memory_space=pltpu.VMEM)
    return pl.pallas_call(
        settle,
        out_shape=jax.ShapeDtypeStruct((rows, depth), F32),
        in_specs=[vmem],
        out_specs=vmem,
        scratch_shapes=[
            pltpu.VMEM((2, 6, SIDE, lot, half), BF16),
            pltpu.VMEM((2, 2, SIDE, lot, half), BF16),
            pltpu.VMEM((2, SIDE, rows, half), BF16),
            pltpu.VMEM((2, 3, rows, half), BF16),
            pltpu.SemaphoreType.DMA((18,)),
            pltpu.SemaphoreType.DMA((18,)),
        ],
        compiler_params=pltpu.CompilerParams(collective_id=2, has_side_effects=True),
        name="settle",
    )(parts)


WAVE = 256
DEPTH = 8
ORDER = (5, 4, 3, 2, 1, 0, 6)
KINDS = (("swap", 0), ("cross", 4), ("cross", 2)) + tuple(
    (name, step)
    for name in ("far", "direct", "summed", "round", "relay", "cross")
    for step in (1, 3)
)


def route(me, base, codes, pos, val, table, most):
    experts = pos.shape[0]
    peers, _, rows = codes.shape
    code = jnp.concatenate([codes[p] for p in range(peers)], axis=1)
    tri = (
        lax.broadcasted_iota(I32, (256, 256), 0) < lax.broadcasted_iota(I32, (256, 256), 1)
    ).astype(BF16)
    carry = jnp.zeros((experts, 1), F32)
    for c in range(peers * rows // 256):
        span = slice(c * 256, (c + 1) * 256)
        local = (code[:, span] >> 4) - me[0] * experts
        gates = (code[:, span] & 15).astype(F32)
        total = jnp.concatenate(
            [
                jnp.sum(jnp.where(local == e, gates, 0.0), axis=0, keepdims=True)
                for e in range(experts)
            ],
            axis=0,
        )
        chosen = (total > 0).astype(F32)
        before = jnp.dot(chosen.astype(BF16), tri, preferred_element_type=F32) + carry
        carry = carry + jnp.sum(chosen, axis=1, keepdims=True)
        val[:, span] = total
        pos[:, span] = jnp.where(total > 0, before, -1e6).astype(I32)
    sizes = (carry.astype(I32) + TILE - 1) // TILE * TILE
    row_of = lax.broadcasted_iota(I32, (experts, 1), 0)
    starts = jnp.zeros((experts, 1), I32)
    for e in range(experts - 1):
        starts = starts + jnp.where(row_of > e, sizes[e : e + 1, :], 0)
    pos[...] += starts - base[0]
    slot = lax.broadcasted_iota(I32, (experts, 128), 1) * TILE + base[0]
    past = jnp.where(starts + sizes <= slot, 1, 0)
    table[...] = jnp.minimum(jnp.sum(past, axis=0, keepdims=True), experts - 1)
    named = jnp.zeros((peers, experts), F32)
    owner_of = lax.broadcasted_iota(I32, (peers, code.shape[1]), 0)
    local_of = lax.broadcasted_iota(I32, (experts, code.shape[1]), 0)
    for k in range(code.shape[0]):
        expert = code[k : k + 1, :] >> 4
        owner = lax.div(expert, experts)
        named = named + lax.dot_general(
            (owner == owner_of).astype(F32).astype(BF16),
            (expert - owner * experts == local_of).astype(F32).astype(BF16),
            (((1,), (1,)), ((), ())),
            preferred_element_type=F32,
        )
    padded = (named.astype(I32) + TILE - 1) // TILE * TILE
    load = jnp.max(jnp.sum(padded, axis=1, keepdims=True), axis=0, keepdims=True)
    most[...] = jnp.broadcast_to(load, most.shape)


def call_route(me, base, codes, experts):
    peers, _, rows = codes.shape
    smem = pl.BlockSpec(memory_space=pltpu.SMEM)
    vmem = pl.BlockSpec(memory_space=pltpu.VMEM)
    return pl.pallas_call(
        route,
        out_shape=(
            jax.ShapeDtypeStruct((experts, peers * rows), I32),
            jax.ShapeDtypeStruct((experts, peers * rows), F32),
            jax.ShapeDtypeStruct((1, 128), I32),
            jax.ShapeDtypeStruct((1, 128), I32),
        ),
        in_specs=[smem, smem, vmem],
        out_specs=(vmem, vmem, vmem, vmem),
        name="route",
    )(me, base, codes)


def core(
    waves,
    table,
    pos,
    val,
    tokens,
    gate_up,
    down,
    out,
    wide,
    narrow,
    wsems,
    hot,
    scale,
    picked,
    parts,
    other,
    far,
    direct,
    summed,
    fill,
    hidden,
    turned,
    acc,
    sends,
    recvs,
):
    me = lax.axis_index("fsdp")
    y, core_at = lax.div(me, 2), lax.rem(me, 2)
    experts, units = down.shape[0], down.shape[2]
    rows = WAVE // 8
    side = WAVE // 2
    tiles = WAVE // TILE
    partner = {"fsdp": y * 2 + 1 - core_at}
    sides = {step: {"fsdp": lax.rem(y + step, SIDE) * 2 + core_at} for step in (1, 3)}
    loads = []
    for e in range(experts):
        loads.append(pltpu.make_async_copy(gate_up.at[e], wide.at[e], wsems.at[e]))
    for e in range(experts):
        loads.append(pltpu.make_async_copy(down.at[e], narrow.at[e], wsems.at[experts + e]))
    for load in loads:
        load.start()
    greet([partner, sides[1], sides[3]])
    columns = (pl.ds(0, units), pl.ds(units, units))

    def half(which):
        return pl.ds(pl.multiple_of(which * side, side), side)

    def block(step):
        at = core_at * side + lax.rem(y + step, SIDE) * rows
        return pl.ds(pl.multiple_of(at, rows), rows)

    def mine(w, step, piece):
        return parts.at[w, block(step), columns[piece]]

    def route_of(kind, w):
        name, step = kind
        piece = LOW if (step == 1) == (name != "direct") else HIGH
        if name == "swap":
            return parts.at[w, half(1 - core_at)], other.at[w], partner
        if name == "far":
            return mine(w, 2, piece), far.at[w, piece], sides[step]
        if name == "direct":
            return mine(w, step, piece), direct.at[w, piece], sides[step]
        if name == "summed":
            return fill.at[w, piece], summed.at[w, piece], sides[step]
        if name == "round":
            own = hidden.at[w, block(0)]
            return own, own, sides[step]
        if name == "cross":
            whole = hidden.at[w, block(4 - step)]
            return whole, whole, partner
        at = core_at * side + lax.rem(y + 4 - step, SIDE) * rows + (step // 2) * (rows // 2)
        part = hidden.at[w, pl.ds(pl.multiple_of(at, rows // 2), rows // 2)]
        return part, part, sides[step]

    def copy(name, step, w):
        src, dst, to = route_of((name, step), w)
        k = KINDS.index((name, step))
        return pltpu.make_async_remote_copy(
            src_ref=src,
            dst_ref=dst,
            send_sem=sends.at[w, k],
            recv_sem=recvs.at[w, k],
            device_id=to,
            device_id_type=MESH,
        )

    slot = lax.broadcasted_iota(I32, (TILE, pos.shape[1]), 0)

    def produce(w):
        spot = lax.rem(w, DEPTH)

        def mark(j, _):
            e = table[w * tiles + j]
            at = pl.multiple_of(j * TILE, TILE)
            same = pos[pl.ds(e, 1), :] - (w * WAVE + at) == slot
            hot[spot, pl.ds(at, TILE), :] = jnp.where(same, 1.0, 0.0).astype(BF16)
            scale[spot, pl.ds(at, TILE), :] = jnp.sum(
                jnp.where(same, val[pl.ds(e, 1), :], 0.0), axis=1, keepdims=True
            )
            return 0

        lax.fori_loop(0, tiles, mark, 0)
        picked[...] = jnp.dot(hot[spot], tokens[...], preferred_element_type=F32).astype(BF16)

        @pl.when(w == 0)
        def _():
            for load in loads[:experts]:
                load.wait()

        def tile(which, j, _):
            j = which * (tiles // 2) + j
            e = table[w * tiles + j]
            at = pl.ds(pl.multiple_of(j * TILE, TILE), TILE)
            parts[w, at, :] = jnp.dot(
                picked[at, :], wide[e], preferred_element_type=F32
            ).astype(BF16)
            return 0

        lax.fori_loop(0, tiles // 2, functools.partial(tile, 1 - core_at), 0)
        copy("swap", 0, w).start()
        lax.fori_loop(0, tiles // 2, functools.partial(tile, core_at), 0)

    def fold(w, step):
        at = pl.ds(pl.multiple_of(lax.rem(y + step, SIDE) * rows, rows), rows)
        parts[w, block(step), :] = parts[w, block(step), :] + other[w, at, :]

    def first(w):
        copy("swap", 0, w).wait_recv()
        fold(w, 2)
        copy("far", 1, w).start()
        copy("far", 3, w).start()
        fold(w, 1)
        copy("direct", 1, w).start()
        fold(w, 3)
        copy("direct", 3, w).start()
        fold(w, 0)

    def second(w):
        for piece, step in ((LOW, 1), (HIGH, 3)):
            copy("far", step, w).wait_recv()
            fill[w, piece] = mine(w, step, piece)[...] + far[w, piece]
            copy("summed", step, w).start()

    def third(w):
        both = []
        for piece, step in ((LOW, 1), (HIGH, 3)):
            copy("direct", 4 - step, w).wait_recv()
            copy("summed", step, w).wait_recv()
            both.append(
                mine(w, 0, piece)[...].astype(F32)
                + direct[w, piece].astype(F32)
                + summed[w, piece].astype(F32)
            )
        gate, up = both
        hidden[w, block(0), :] = (gate / (1 + jnp.exp(-gate)) * up).astype(BF16)
        copy("round", 1, w).start()
        copy("round", 3, w).start()
        copy("cross", 4, w).start()

    def fourth(w):
        for step in (1, 3):
            copy("round", step, w).wait_recv()
            copy("relay", step, w).start()
            copy("cross", step, w).start()

    def fifth(w):
        for step in (1, 3):
            copy("relay", step, w).wait_recv()
        copy("cross", 2, w).start()

    def consume(w):
        spot = lax.rem(w, DEPTH)

        @pl.when(w == 0)
        def _():
            for load in loads[experts:]:
                load.wait()

        for step in (4, 1, 3, 2):
            copy("cross", step, w).wait_recv()

        def tile(j, _):
            e = table[w * tiles + j]
            at = pl.ds(pl.multiple_of(j * TILE, TILE), TILE)
            result = lax.dot_general(
                hidden[w, at, :], narrow[e], (((1,), (1,)), ((), ())), preferred_element_type=F32
            )
            turned[at, :] = result * scale[spot, at, :]
            return 0

        lax.fori_loop(0, tiles, tile, 0)
        flat = turned[...].T.astype(BF16)
        for c in range(pos.shape[1] // LANES):
            lane = pl.ds(c * LANES, LANES)
            acc[:, lane] += jnp.dot(flat, hot[spot, :, lane], preferred_element_type=F32)

    acc[...] = jnp.zeros_like(acc)
    stages = (produce, first, second, third, fourth, fifth, consume)

    def turn(t, _):
        for late in ORDER:
            w = t - late

            @pl.when((w >= 0) & (w < waves))
            def _(late=late, w=w):
                stages[late](w)

        return 0

    lax.fori_loop(0, waves + len(stages) - 1, turn, 0)

    def flip(c, _):
        lane = pl.multiple_of(c * 256, 256)
        out[pl.ds(lane, 256), :] = acc[:, pl.ds(lane, 256)].T.astype(out.dtype)
        return 0

    lax.fori_loop(0, out.shape[0] // 256, flip, 0)

    def drain(w, _):
        for name, step in KINDS:
            copy(name, step, w).wait_send()
        return 0

    lax.fori_loop(0, waves, drain, 0)


def call_core(waves, table, pos, val, tokens, gate_up, down):
    experts, depth, width = gate_up.shape
    rows, units = WAVE // 8, width // 2
    total = tokens.shape[0]
    smem = pl.BlockSpec(memory_space=pltpu.SMEM)
    vmem = pl.BlockSpec(memory_space=pltpu.VMEM)
    hbm = pl.BlockSpec(memory_space=pl.ANY)
    piece = pltpu.VMEM((waves, 2, rows, units), BF16)
    return pl.pallas_call(
        functools.partial(core, waves),
        out_shape=jax.ShapeDtypeStruct((total, depth), BF16),
        in_specs=[smem, vmem, vmem, vmem, hbm, hbm],
        out_specs=vmem,
        scratch_shapes=[
            pltpu.VMEM(gate_up.shape, BF16),
            pltpu.VMEM(down.shape, BF16),
            pltpu.SemaphoreType.DMA((2 * experts,)),
            pltpu.VMEM((DEPTH, WAVE, total), BF16),
            pltpu.VMEM((DEPTH, WAVE, 1), F32),
            pltpu.VMEM((WAVE, depth), BF16),
            pltpu.VMEM((waves, WAVE, width), BF16),
            pltpu.VMEM((waves, WAVE // 2, width), BF16),
            piece,
            piece,
            piece,
            piece,
            pltpu.VMEM((waves, WAVE, units), BF16),
            pltpu.VMEM((WAVE, depth), F32),
            pltpu.VMEM((depth, total), F32),
            pltpu.SemaphoreType.DMA((waves, len(KINDS))),
            pltpu.SemaphoreType.DMA((waves, len(KINDS))),
        ],
        compiler_params=pltpu.CompilerParams(
            collective_id=waves, has_side_effects=True, vmem_limit_bytes=62 << 20
        ),
        name="core%d" % waves,
    )(table, pos, val, tokens, gate_up, down)


def local(tokens, gate_up_weight, down_weight, placement, copy_ids, gate_codes):
    steps, rows, depth = tokens.shape
    experts = gate_up_weight.shape[0]
    top = copy_ids.shape[2]
    peers = lax.axis_size("ep")
    own = lax.axis_index("ep").astype(I32).reshape(1)
    raw = (copy_ids * 16 + gate_codes).reshape(steps * rows, top).T
    codes, everyone = call_share(raw, placement, tokens.reshape(steps * rows, depth))
    codes = codes.reshape(peers, top, steps * rows)
    everyone = everyone.reshape(peers * steps * rows, depth)

    def chunk(base, waves):
        pos, val, table, _ = call_route(own, base.reshape(1), codes, experts)
        return call_core(waves, table.reshape(-1), pos, val, everyone, gate_up_weight, down_weight)

    pos, val, table, most = call_route(own, jnp.zeros((1,), I32), codes, experts)
    most = most[0, 0]
    branches = [functools.partial(call_core, waves) for waves in CHOICES]
    pick = jnp.int32(0)
    for waves in CHOICES[:-1]:
        pick += (most > waves * WAVE).astype(I32)
    mixed = lax.switch(
        pick, branches, table.reshape(-1), pos, val, everyone, gate_up_weight, down_weight
    )
    span = CHOICES[-1] * WAVE
    _, mixed = lax.while_loop(
        lambda c: c[0] * span < most,
        lambda c: (
            c[0] + 1,
            (c[1].astype(F32) + chunk(c[0] * span, CHOICES[-1]).astype(F32)).astype(BF16),
        ),
        (jnp.int32(1), mixed),
    )
    mixed = call_settle(mixed.reshape(SIDE, SIDE, steps * rows, depth))
    total = jnp.sum(gate_codes, axis=2).astype(F32)
    return (mixed.reshape(steps, rows, depth) / total[:, :, None]).astype(BF16)


def solution(mesh):
    in_specs = (
        P(None, "ep", "fsdp"),
        P("ep", "fsdp", None),
        P("ep", "fsdp", None),
        P(),
        P(None, "ep", None),
        P(None, "ep", None),
    )
    out_specs = P(None, "ep", "fsdp")
    return jax.shard_map(local, mesh=mesh, in_specs=in_specs, out_specs=out_specs, check_vma=False)
```

```python
import functools

import jax
import jax.numpy as jnp
from jax import lax
from jax.experimental import pallas as pl
from jax.experimental.pallas import tpu as pltpu
from jax.sharding import PartitionSpec as P

I32, F32, BF16 = jnp.int32, jnp.float32, jnp.bfloat16
TILE = 32
LANES = 512
TABLE = 512
CHOICES = (7, 8, 9, 10)
MESH = pl.DeviceIdType.MESH
SIDE = 4
LOW, HIGH = 0, 1


class Post:
    def __init__(self, sends, recvs):
        self.sends, self.recvs, self.made = sends, recvs, {}

    def send(self, key, src, dst, target):
        number = self.made.setdefault(key, len(self.made))
        copy = pltpu.make_async_remote_copy(
            src_ref=src,
            dst_ref=dst,
            send_sem=self.sends.at[number],
            recv_sem=self.recvs.at[number],
            device_id=target,
            device_id_type=MESH,
        )
        copy.start()
        self.made[key] = number
        setattr(self, "copy_%d" % number, copy)

    def arrived(self, key):
        getattr(self, "copy_%d" % self.made[key]).wait_recv()

    def drain(self):
        for number in self.made.values():
            getattr(self, "copy_%d" % number).wait_send()


def greet(targets):
    barrier = pltpu.get_barrier_semaphore()
    for target in targets:
        pl.semaphore_signal(barrier, inc=1, device_id=target, device_id_type=MESH)
    pl.semaphore_wait(barrier, len(targets))


def torus():
    me = lax.axis_index("ep")
    z, x = lax.div(me, SIDE), lax.rem(me, SIDE)

    def at(dz, dx):
        return lax.rem(z + dz, SIDE) * SIDE + lax.rem(x + dx, SIDE)

    return me, z, x, at


def routing(me, pieces, pos, val, table, most):
    experts = pos.shape[0]
    peers = SIDE * SIDE
    code = jnp.concatenate(pieces, axis=1)
    tri = (
        lax.broadcasted_iota(I32, (256, 256), 0) < lax.broadcasted_iota(I32, (256, 256), 1)
    ).astype(F32).astype(BF16)
    carry = jnp.zeros((experts, 1), F32)
    for c in range(code.shape[1] // 256):
        span = slice(c * 256, (c + 1) * 256)
        local = (code[:, span] >> 4) - me * experts
        gates = (code[:, span] & 15).astype(F32)
        total = jnp.concatenate(
            [
                jnp.sum(jnp.where(local == e, gates, 0.0), axis=0, keepdims=True)
                for e in range(experts)
            ],
            axis=0,
        )
        chosen = (total > 0).astype(F32)
        before = jnp.dot(chosen.astype(BF16), tri, preferred_element_type=F32) + carry
        carry = carry + jnp.sum(chosen, axis=1, keepdims=True)
        val[:, span] = total
        pos[:, span] = jnp.where(total > 0, before, -1e6).astype(I32)
    sizes = (carry.astype(I32) + TILE - 1) // TILE * TILE
    row_of = lax.broadcasted_iota(I32, (experts, 1), 0)
    starts = jnp.zeros((experts, 1), I32)
    for e in range(experts - 1):
        starts = starts + jnp.where(row_of > e, sizes[e : e + 1, :], 0)
    pos[...] += starts
    slot = lax.broadcasted_iota(I32, (experts, table.shape[1]), 1) * TILE
    past = jnp.where(starts + sizes <= slot, 1, 0)
    table[...] = jnp.minimum(jnp.sum(past, axis=0, keepdims=True), experts - 1)
    named = jnp.zeros((peers, experts), F32)
    owner_of = lax.broadcasted_iota(I32, (peers, code.shape[1]), 0)
    local_of = lax.broadcasted_iota(I32, (experts, code.shape[1]), 0)
    for k in range(code.shape[0]):
        expert = code[k : k + 1, :] >> 4
        owner = lax.div(expert, experts)
        named = named + lax.dot_general(
            (owner == owner_of).astype(F32).astype(BF16),
            (expert - owner * experts == local_of).astype(F32).astype(BF16),
            (((1,), (1,)), ((), ())),
            preferred_element_type=F32,
        )
    padded = (named.astype(I32) + TILE - 1) // TILE * TILE
    load = jnp.max(jnp.sum(padded, axis=1, keepdims=True), axis=0, keepdims=True)
    most[...] = jnp.broadcast_to(load, most.shape)


def share(
    ids,
    gates,
    placement,
    tokens,
    tokens_all,
    pos,
    val,
    table,
    most,
    totals,
    codes_all,
    keep,
    sends,
    recvs,
):
    me, z, x, at = torus()
    barrier = pltpu.get_barrier_semaphore()
    peers = [(0, step) for step in (1, 2, 3)] + [(step, 0) for step in (1, 2, 3)]
    for dz, dx in peers:
        pl.semaphore_signal(barrier, inc=1, device_id={"ep": at(dz, dx)}, device_id_type=MESH)
    copies = ids[...]

    def look(i, found):
        return jnp.where(copies == i, placement[i], found)

    found = lax.fori_loop(0, placement.shape[0], look, jnp.zeros_like(copies), unroll=8)
    codes_all[z, x] = found * 16 + gates[...]
    totals[...] = jnp.sum(gates[...].astype(F32), axis=1)
    codes = codes_all.at[z, x]
    pl.semaphore_wait(barrier, len(peers))
    rows, depth = tokens.shape
    half = depth // 2
    post = Post(sends, recvs)
    for step in (1, 3, 2):
        post.send(("codes", 1, step), codes, codes_all.at[z, x], {"ep": at(0, step)})

    def place(side, first, second):
        return at(second, first) if side == 0 else at(first, second)

    def block(side, first, second, part=None):
        span = slice(None) if part is None else pl.ds(part * (rows // 2), rows // 2)
        return tokens_all.at[place(side, first, second), span, pl.ds(side * half, half)]

    def target(side, axis, step):
        first, second = (step, 0) if axis == 1 else (0, step)
        return {"ep": place(side, first, second)}

    for axis, steps in ((1, (2, 1, 3)), (2, (1, 3))):
        for side in (0, 1):
            own = tokens.at[:, pl.ds(side * half, half)]
            for step in steps:
                post.send((side, axis, 0, step), own, block(side, 0, 0), target(side, axis, step))
    mine = pltpu.make_async_copy(tokens, tokens_all.at[me], keep.at[0])
    mine.start()

    def onward(side, first, steps):
        src = block(side, first, 0)
        for step in steps:
            post.send((side, 2, first, step), src, src, target(side, 2, step))

    def relay(side, first):
        for step in (1, 3):
            post.arrived((side, 2, first, step))
            part = LOW if step == 1 else HIGH
            src = block(side, first, 4 - step, part)
            post.send((side, 2, first, "far", step), src, src, target(side, 2, step))

    for step in (1, 3, 2):
        post.arrived(("codes", 1, step))
    for step in (1, 3, 2):
        post.send(("codes", 2, step), codes_all.at[z], codes_all.at[z], {"ep": at(step, 0)})
    for step in (1, 3):
        for side in (0, 1):
            post.arrived((side, 1, 0, step))
            onward(side, 4 - step, (1, 3))
    for side in (0, 1):
        post.arrived((side, 1, 0, 2))
        onward(side, 2, (2, 1, 3))
    for first in (0, 3, 1):
        for side in (0, 1):
            relay(side, first)
    for step in (1, 3, 2):
        post.arrived(("codes", 2, step))
    pieces = [
        codes_all[far, near, step]
        for far in range(SIDE)
        for near in range(SIDE)
        for step in range(ids.shape[0])
    ]
    routing(me, pieces, pos, val, table, most)
    for first in (0, 3, 1):
        for side in (0, 1):
            for step in (1, 3):
                post.arrived((side, 2, first, "far", step))
    for side in (0, 1):
        for step in (1, 3, 2):
            post.arrived((side, 2, 2, step))
    post.drain()
    mine.wait()


def call_share(ids, gates, placement, tokens, experts):
    vmem = pl.BlockSpec(memory_space=pltpu.VMEM)
    smem = pl.BlockSpec(memory_space=pltpu.SMEM)
    hbm = pl.BlockSpec(memory_space=pl.ANY)
    peers = SIDE * SIDE
    total = peers * tokens.shape[0]
    return pl.pallas_call(
        share,
        out_shape=(
            jax.ShapeDtypeStruct((peers,) + tokens.shape, tokens.dtype),
            jax.ShapeDtypeStruct((experts, total), I32),
            jax.ShapeDtypeStruct((experts, total), F32),
            jax.ShapeDtypeStruct((1, TABLE), I32),
            jax.ShapeDtypeStruct((1, 128), I32),
            jax.ShapeDtypeStruct((ids.shape[0], ids.shape[2]), F32),
        ),
        in_specs=[vmem, vmem, smem, vmem],
        out_specs=(hbm, vmem, vmem, vmem, vmem, vmem),
        scratch_shapes=[
            pltpu.VMEM((SIDE, SIDE) + ids.shape, ids.dtype),
            pltpu.SemaphoreType.DMA((1,)),
            pltpu.SemaphoreType.DMA((42,)),
            pltpu.SemaphoreType.DMA((42,)),
        ],
        compiler_params=pltpu.CompilerParams(collective_id=1, has_side_effects=True),
        name="share",
    )(ids, gates, placement, tokens)


def settle(parts, out, big, fills, sums, small, sends, recvs):
    me, z, x, at = torus()
    greet([{"ep": at(0, step)} for step in (1, 2, 3)] + [{"ep": at(step, 0)} for step in (1, 2, 3)])
    rows, depth = parts.shape[2:]
    half, lot = depth // 2, rows // 2
    post = Post(sends, recvs)
    axis_one = (x, z)
    axis_two = (z, x)

    def wide(side, step, part):
        to = lax.rem(axis_one[side] + step, SIDE)
        spot = (slice(None), to) if side == 0 else (to, slice(None))
        return parts.at[spot + (pl.ds(part * lot, lot), pl.ds(side * half, half))]

    def target(side, stage, step):
        along_x = (side == 0) == (stage == 1)
        return {"ep": at(0, step) if along_x else at(step, 0)}

    for side in (0, 1):
        post.send((side, 0), wide(side, 2, LOW), big.at[side, 0], target(side, 1, 1))
        post.send((side, 1), wide(side, 2, HIGH), big.at[side, 1], target(side, 1, 3))
    for side in (0, 1):
        post.send((side, 3), wide(side, 1, HIGH), big.at[side, 3], target(side, 1, 1))
        post.send((side, 2), wide(side, 3, LOW), big.at[side, 2], target(side, 1, 3))
    for side in (0, 1):
        for part, step in ((LOW, 1), (HIGH, 3)):
            post.arrived((side, part))
            fills[side, part] = wide(side, step, part)[...] + big[side, part]
            post.send((side, 4 + part), fills.at[side, part], big.at[side, 4 + part], target(side, 1, step))
    for side in (0, 1):
        for part in (HIGH, LOW):
            post.arrived((side, 2 + part))
            post.arrived((side, 4 + part))
            sums[side, :, pl.ds(part * lot, lot), :] = (
                wide(side, 0, part)[...].astype(F32)
                + big[side, 2 + part].astype(F32)
                + big[side, 4 + part].astype(F32)
            ).astype(BF16)
        for step in (2, 1, 3):
            to = lax.rem(axis_two[side] + step, SIDE)
            post.send((side, "two", step), sums.at[side, to], small.at[side, step - 1], target(side, 2, step))
    for side in (0, 1):
        for step in (1, 3, 2):
            post.arrived((side, "two", step))
        out[:, pl.ds(side * half, half)] = (
            sums[side, axis_two[side]].astype(F32)
            + small[side, 0].astype(F32)
            + small[side, 1].astype(F32)
            + small[side, 2].astype(F32)
        )
    post.drain()


def call_settle(parts):
    rows, depth = parts.shape[2:]
    lot, half = rows // 2, depth // 2
    vmem = pl.BlockSpec(memory_space=pltpu.VMEM)
    return pl.pallas_call(
        settle,
        out_shape=jax.ShapeDtypeStruct((rows, depth), F32),
        in_specs=[vmem],
        out_specs=vmem,
        scratch_shapes=[
            pltpu.VMEM((2, 6, SIDE, lot, half), BF16),
            pltpu.VMEM((2, 2, SIDE, lot, half), BF16),
            pltpu.VMEM((2, SIDE, rows, half), BF16),
            pltpu.VMEM((2, 3, rows, half), BF16),
            pltpu.SemaphoreType.DMA((18,)),
            pltpu.SemaphoreType.DMA((18,)),
        ],
        compiler_params=pltpu.CompilerParams(collective_id=2, has_side_effects=True),
        name="settle",
    )(parts)


WAVE = 256
DEPTH = 7
ORDER = (5, 4, 3, 2, 1, 0, 6)
KINDS = (("swap", 0), ("cross", 4), ("cross", 2)) + tuple(
    (name, step)
    for name in ("far", "direct", "summed", "round", "relay", "cross")
    for step in (1, 3)
)


def core(
    waves,
    table,
    pos,
    val,
    tokens,
    gate_up,
    down,
    out,
    wide,
    narrow,
    flipped,
    wsems,
    hot,
    plain,
    picked,
    parts,
    other,
    far,
    direct,
    summed,
    fill,
    hidden,
    turned,
    acc,
    sends,
    recvs,
):
    me = lax.axis_index("fsdp")
    y, core_at = lax.div(me, 2), lax.rem(me, 2)
    experts, units = down.shape[0], down.shape[2]
    rows = WAVE // 8
    side = WAVE // 2
    tiles = WAVE // TILE
    partner = {"fsdp": y * 2 + 1 - core_at}
    sides = {step: {"fsdp": lax.rem(y + step, SIDE) * 2 + core_at} for step in (1, 3)}
    loads = []
    for e in range(experts):
        loads.append(pltpu.make_async_copy(gate_up.at[e], wide.at[e], wsems.at[e]))
    for e in range(experts):
        loads.append(pltpu.make_async_copy(down.at[e], narrow.at[e], wsems.at[experts + e]))
    for load in loads:
        load.start()
    greet([partner, sides[1], sides[3]])
    columns = (pl.ds(0, units), pl.ds(units, units))

    def half(which):
        return pl.ds(pl.multiple_of(which * side, side), side)

    def block(step):
        at = core_at * side + lax.rem(y + step, SIDE) * rows
        return pl.ds(pl.multiple_of(at, rows), rows)

    def mine(w, step, piece):
        return parts.at[w, block(step), columns[piece]]

    def route_of(kind, w):
        name, step = kind
        piece = LOW if (step == 1) == (name != "direct") else HIGH
        if name == "swap":
            return parts.at[w, half(1 - core_at)], other.at[w], partner
        if name == "far":
            return mine(w, 2, piece), far.at[w, piece], sides[step]
        if name == "direct":
            return mine(w, step, piece), direct.at[w, piece], sides[step]
        if name == "summed":
            return fill.at[w, piece], summed.at[w, piece], sides[step]
        if name == "round":
            own = hidden.at[w, block(0)]
            return own, own, sides[step]
        if name == "cross":
            whole = hidden.at[w, block(4 - step)]
            return whole, whole, partner
        at = core_at * side + lax.rem(y + 4 - step, SIDE) * rows + (step // 2) * (rows // 2)
        part = hidden.at[w, pl.ds(pl.multiple_of(at, rows // 2), rows // 2)]
        return part, part, sides[step]

    def copy(name, step, w):
        src, dst, to = route_of((name, step), w)
        k = KINDS.index((name, step))
        return pltpu.make_async_remote_copy(
            src_ref=src,
            dst_ref=dst,
            send_sem=sends.at[w, k],
            recv_sem=recvs.at[w, k],
            device_id=to,
            device_id_type=MESH,
        )

    slot = lax.broadcasted_iota(I32, (TILE, pos.shape[1]), 0)

    def produce(w):
        spot = lax.rem(w, DEPTH)

        def mark(j, _):
            e = table[w * tiles + j]
            at = pl.multiple_of(j * TILE, TILE)
            same = pos[pl.ds(e, 1), :] - (w * WAVE + at) == slot
            plain[pl.ds(at, TILE), :] = jnp.where(same, 1.0, 0.0).astype(BF16)
            hot[spot, pl.ds(at, TILE), :] = jnp.where(same, val[pl.ds(e, 1), :], 0.0).astype(BF16)
            return 0

        lax.fori_loop(0, tiles, mark, 0)
        picked[...] = jnp.dot(plain[...], tokens[...], preferred_element_type=F32).astype(BF16)

        @pl.when(w == 0)
        def _():
            for load in loads[:experts]:
                load.wait()

        def tile(which, j, _):
            j = which * (tiles // 2) + j
            e = table[w * tiles + j]
            at = pl.ds(pl.multiple_of(j * TILE, TILE), TILE)
            parts[w, at, :] = jnp.dot(
                picked[at, :], wide[e], preferred_element_type=F32
            ).astype(BF16)
            return 0

        lax.fori_loop(0, tiles // 2, functools.partial(tile, 1 - core_at), 0, unroll=True)
        copy("swap", 0, w).start()
        lax.fori_loop(0, tiles // 2, functools.partial(tile, core_at), 0, unroll=True)

    def fold(w, step):
        at = pl.ds(pl.multiple_of(lax.rem(y + step, SIDE) * rows, rows), rows)
        parts[w, block(step), :] = parts[w, block(step), :] + other[w, at, :]

    def first(w):
        copy("swap", 0, w).wait_recv()
        fold(w, 2)
        copy("far", 1, w).start()
        copy("far", 3, w).start()
        fold(w, 1)
        copy("direct", 1, w).start()
        fold(w, 3)
        copy("direct", 3, w).start()
        fold(w, 0)

    def second(w):
        for piece, step in ((LOW, 1), (HIGH, 3)):
            copy("far", step, w).wait_recv()
            fill[w, piece] = mine(w, step, piece)[...] + far[w, piece]
            copy("summed", step, w).start()

    def third(w):
        both = []
        for piece, step in ((LOW, 1), (HIGH, 3)):
            copy("direct", 4 - step, w).wait_recv()
            copy("summed", step, w).wait_recv()
            both.append(
                mine(w, 0, piece)[...].astype(F32)
                + direct[w, piece].astype(F32)
                + summed[w, piece].astype(F32)
            )
        gate, up = both
        hidden[w, block(0), :] = (gate / (1 + jnp.exp(-gate)) * up).astype(BF16)
        copy("round", 1, w).start()
        copy("round", 3, w).start()
        copy("cross", 4, w).start()

    def fourth(w):
        for step in (1, 3):
            copy("round", step, w).wait_recv()
            copy("relay", step, w).start()
            copy("cross", step, w).start()

    def fifth(w):
        for step in (1, 3):
            copy("relay", step, w).wait_recv()
        copy("cross", 2, w).start()

    def consume(w):
        spot = lax.rem(w, DEPTH)
        for step in (4, 1, 3, 2):
            copy("cross", step, w).wait_recv()

        def tile(j, _):
            e = table[w * tiles + j]
            at = pl.ds(pl.multiple_of(j * TILE, TILE), TILE)
            turned[at, :] = jnp.dot(hidden[w, at, :], flipped[e], preferred_element_type=F32)
            return 0

        lax.fori_loop(0, tiles, tile, 0, unroll=True)
        flat = turned[...].T.astype(BF16)
        for c in range(pos.shape[1] // LANES):
            lane = pl.ds(c * LANES, LANES)
            acc[:, lane] += jnp.dot(flat, hot[spot, :, lane], preferred_element_type=F32)

    acc[...] = jnp.zeros_like(acc)
    stages = (produce, first, second, third, fourth, fifth, consume)

    def turn(t, _):
        for late in ORDER:
            w = t - late

            @pl.when((w >= 0) & (w < waves))
            def _(late=late, w=w):
                stages[late](w)

        @pl.when(t == 0)
        def _():
            for load in loads[experts:]:
                load.wait()

        @pl.when(t < 4)
        def _():
            for e in (2 * t, 2 * t + 1):
                flipped[e] = narrow[e].astype(F32).T.astype(BF16)

        return 0

    lax.fori_loop(0, waves + len(stages) - 1, turn, 0)

    def flip(c, _):
        lane = pl.multiple_of(c * 256, 256)
        out[pl.ds(lane, 256), :] = acc[:, pl.ds(lane, 256)].T.astype(out.dtype)
        return 0

    lax.fori_loop(0, out.shape[0] // 256, flip, 0)

    def drain(w, _):
        for name, step in KINDS:
            copy(name, step, w).wait_send()
        return 0

    lax.fori_loop(0, waves, drain, 0)


def call_core(waves, table, pos, val, tokens, gate_up, down):
    experts, depth, width = gate_up.shape
    rows, units = WAVE // 8, width // 2
    total = tokens.shape[0]
    smem = pl.BlockSpec(memory_space=pltpu.SMEM)
    vmem = pl.BlockSpec(memory_space=pltpu.VMEM)
    hbm = pl.BlockSpec(memory_space=pl.ANY)
    piece = pltpu.VMEM((waves, 2, rows, units), BF16)
    return pl.pallas_call(
        functools.partial(core, waves),
        out_shape=jax.ShapeDtypeStruct((total, depth), BF16),
        in_specs=[smem, vmem, vmem, vmem, hbm, hbm],
        out_specs=vmem,
        scratch_shapes=[
            pltpu.VMEM(gate_up.shape, BF16),
            pltpu.VMEM(down.shape, BF16),
            pltpu.VMEM((experts, units, depth), BF16),
            pltpu.SemaphoreType.DMA((2 * experts,)),
            pltpu.VMEM((DEPTH, WAVE, total), BF16),
            pltpu.VMEM((WAVE, total), BF16),
            pltpu.VMEM((WAVE, depth), BF16),
            pltpu.VMEM((waves, WAVE, width), BF16),
            pltpu.VMEM((waves, WAVE // 2, width), BF16),
            piece,
            piece,
            piece,
            piece,
            pltpu.VMEM((waves, WAVE, units), BF16),
            pltpu.VMEM((WAVE, depth), F32),
            pltpu.VMEM((depth, total), F32),
            pltpu.SemaphoreType.DMA((waves, len(KINDS))),
            pltpu.SemaphoreType.DMA((waves, len(KINDS))),
        ],
        compiler_params=pltpu.CompilerParams(
            collective_id=waves, has_side_effects=True, vmem_limit_bytes=62 << 20
        ),
        name="core%d" % waves,
    )(table, pos, val, tokens, gate_up, down)


def local(tokens, gate_up_weight, down_weight, placement, copy_ids, gate_codes):
    steps, rows, depth = tokens.shape
    experts = gate_up_weight.shape[0]
    peers = lax.axis_size("ep")
    everyone, pos, val, table, most, totals = call_share(
        copy_ids.transpose(0, 2, 1),
        gate_codes.transpose(0, 2, 1),
        placement,
        tokens.reshape(steps * rows, depth),
        experts,
    )
    everyone = everyone.reshape(peers * steps * rows, depth)
    most = most[0, 0]
    table = table.reshape(-1)
    tiles = CHOICES[-1] * WAVE // TILE

    def chunk(base, waves):
        part = lax.dynamic_slice(table, (base // TILE,), (tiles,))
        return call_core(waves, part, pos - base, val, everyone, gate_up_weight, down_weight)

    branches = [functools.partial(call_core, waves) for waves in CHOICES]
    pick = jnp.int32(0)
    for waves in CHOICES[:-1]:
        pick += (most > waves * WAVE).astype(I32)
    mixed = lax.switch(
        pick, branches, table[:tiles], pos, val, everyone, gate_up_weight, down_weight
    )
    span = CHOICES[-1] * WAVE
    _, mixed = lax.while_loop(
        lambda c: c[0] * span < most,
        lambda c: (
            c[0] + 1,
            (c[1].astype(F32) + chunk(c[0] * span, CHOICES[-1]).astype(F32)).astype(BF16),
        ),
        (jnp.int32(1), mixed),
    )
    mixed = call_settle(mixed.reshape(SIDE, SIDE, steps * rows, depth))
    return (mixed.reshape(steps, rows, depth) / totals[:, :, None]).astype(BF16)


def solution(mesh):
    in_specs = (
        P(None, "ep", "fsdp"),
        P("ep", "fsdp", None),
        P("ep", "fsdp", None),
        P(),
        P(None, "ep", None),
        P(None, "ep", None),
    )
    out_specs = P(None, "ep", "fsdp")
    return jax.shard_map(local, mesh=mesh, in_specs=in_specs, out_specs=out_specs, check_vma=False)
```

```python
import functools

import jax
import jax.numpy as jnp
from jax import lax
from jax.experimental import pallas as pl
from jax.experimental.pallas import tpu as pltpu
from jax.sharding import PartitionSpec as P

I32, F32, BF16 = jnp.int32, jnp.float32, jnp.bfloat16
TILE = 32
LANES = 512
TABLE = 512
CHOICES = (7, 8, 9, 10)
MESH = pl.DeviceIdType.MESH
SIDE = 4
LOW, HIGH = 0, 1


class Post:
    def __init__(self, sends, recvs):
        self.sends, self.recvs, self.made = sends, recvs, {}

    def send(self, key, src, dst, target):
        number = self.made.setdefault(key, len(self.made))
        copy = pltpu.make_async_remote_copy(
            src_ref=src,
            dst_ref=dst,
            send_sem=self.sends.at[number],
            recv_sem=self.recvs.at[number],
            device_id=target,
            device_id_type=MESH,
        )
        copy.start()
        self.made[key] = number
        setattr(self, "copy_%d" % number, copy)

    def arrived(self, key):
        getattr(self, "copy_%d" % self.made[key]).wait_recv()

    def drain(self):
        for number in self.made.values():
            getattr(self, "copy_%d" % number).wait_send()


def greet(targets):
    barrier = pltpu.get_barrier_semaphore()
    for target in targets:
        pl.semaphore_signal(barrier, inc=1, device_id=target, device_id_type=MESH)
    pl.semaphore_wait(barrier, len(targets))


def torus():
    me = lax.axis_index("ep")
    z, x = lax.div(me, SIDE), lax.rem(me, SIDE)

    def at(dz, dx):
        return lax.rem(z + dz, SIDE) * SIDE + lax.rem(x + dx, SIDE)

    return me, z, x, at


def routing(me, pieces, pos, val, table, most):
    experts = pos.shape[0]
    peers = SIDE * SIDE
    code = jnp.concatenate(pieces, axis=1)
    tri = (
        lax.broadcasted_iota(I32, (256, 256), 0) < lax.broadcasted_iota(I32, (256, 256), 1)
    ).astype(F32).astype(BF16)
    carry = jnp.zeros((experts, 1), F32)
    for c in range(code.shape[1] // 256):
        span = slice(c * 256, (c + 1) * 256)
        local = (code[:, span] >> 4) - me * experts
        gates = (code[:, span] & 15).astype(F32)
        total = jnp.concatenate(
            [
                jnp.sum(jnp.where(local == e, gates, 0.0), axis=0, keepdims=True)
                for e in range(experts)
            ],
            axis=0,
        )
        chosen = (total > 0).astype(F32)
        before = jnp.dot(chosen.astype(BF16), tri, preferred_element_type=F32) + carry
        carry = carry + jnp.sum(chosen, axis=1, keepdims=True)
        val[:, span] = total
        pos[:, span] = jnp.where(total > 0, before, -1e6).astype(I32)
    sizes = (carry.astype(I32) + TILE - 1) // TILE * TILE
    row_of = lax.broadcasted_iota(I32, (experts, 1), 0)
    starts = jnp.zeros((experts, 1), I32)
    for e in range(experts - 1):
        starts = starts + jnp.where(row_of > e, sizes[e : e + 1, :], 0)
    pos[...] += starts
    slot = lax.broadcasted_iota(I32, (experts, table.shape[1]), 1) * TILE
    past = jnp.where(starts + sizes <= slot, 1, 0)
    table[...] = jnp.minimum(jnp.sum(past, axis=0, keepdims=True), experts - 1)
    named = jnp.zeros((peers, experts), F32)
    owner_of = lax.broadcasted_iota(I32, (peers, code.shape[1]), 0)
    local_of = lax.broadcasted_iota(I32, (experts, code.shape[1]), 0)
    every = code >> 4
    again = jnp.zeros(every.shape, I32)
    choice = lax.broadcasted_iota(I32, every.shape, 0)
    for step in range(1, every.shape[0]):
        same = (pltpu.roll(every, step, 0) == every) & (choice >= step)
        again = jnp.where(same, 1, again)
    every = jnp.where(again > 0, peers * experts, every)
    for k in range(code.shape[0]):
        expert = every[k : k + 1, :]
        owner = lax.div(expert, experts)
        named = named + lax.dot_general(
            (owner == owner_of).astype(F32).astype(BF16),
            (expert - owner * experts == local_of).astype(F32).astype(BF16),
            (((1,), (1,)), ((), ())),
            preferred_element_type=F32,
        )
    padded = (named.astype(I32) + TILE - 1) // TILE * TILE
    load = jnp.max(jnp.sum(padded, axis=1, keepdims=True), axis=0, keepdims=True)
    most[...] = jnp.broadcast_to(load, most.shape)


def share(
    ids,
    gates,
    placement,
    tokens,
    tokens_all,
    pos,
    val,
    table,
    most,
    totals,
    codes_all,
    keep,
    sends,
    recvs,
):
    me, z, x, at = torus()
    barrier = pltpu.get_barrier_semaphore()
    peers = [(0, step) for step in (1, 2, 3)] + [(step, 0) for step in (1, 2, 3)]
    for dz, dx in peers:
        pl.semaphore_signal(barrier, inc=1, device_id={"ep": at(dz, dx)}, device_id_type=MESH)
    copies = ids[...]

    def look(i, found):
        return jnp.where(copies == i, placement[i], found)

    found = lax.fori_loop(0, placement.shape[0], look, jnp.zeros_like(copies), unroll=8)
    codes_all[z, x] = found * 16 + gates[...]
    totals[...] = jnp.sum(gates[...].astype(F32), axis=1)
    codes = codes_all.at[z, x]
    pl.semaphore_wait(barrier, len(peers))
    rows, depth = tokens.shape
    half = depth // 2
    post = Post(sends, recvs)
    for step in (1, 3, 2):
        post.send(("codes", 1, step), codes, codes_all.at[z, x], {"ep": at(0, step)})

    def place(side, first, second):
        return at(second, first) if side == 0 else at(first, second)

    def block(side, first, second, part=None):
        span = slice(None) if part is None else pl.ds(part * (rows // 2), rows // 2)
        return tokens_all.at[place(side, first, second), span, pl.ds(side * half, half)]

    def target(side, axis, step):
        first, second = (step, 0) if axis == 1 else (0, step)
        return {"ep": place(side, first, second)}

    for axis, steps in ((1, (2, 1, 3)), (2, (1, 3))):
        for side in (0, 1):
            own = tokens.at[:, pl.ds(side * half, half)]
            for step in steps:
                post.send((side, axis, 0, step), own, block(side, 0, 0), target(side, axis, step))
    mine = pltpu.make_async_copy(tokens, tokens_all.at[me], keep.at[0])
    mine.start()

    def onward(side, first, steps):
        src = block(side, first, 0)
        for step in steps:
            post.send((side, 2, first, step), src, src, target(side, 2, step))

    def relay(side, first):
        for step in (1, 3):
            post.arrived((side, 2, first, step))
            part = LOW if step == 1 else HIGH
            src = block(side, first, 4 - step, part)
            post.send((side, 2, first, "far", step), src, src, target(side, 2, step))

    for step in (1, 3, 2):
        post.arrived(("codes", 1, step))
    for step in (1, 3, 2):
        post.send(("codes", 2, step), codes_all.at[z], codes_all.at[z], {"ep": at(step, 0)})
    for step in (1, 3):
        for side in (0, 1):
            post.arrived((side, 1, 0, step))
            onward(side, 4 - step, (1, 3))
    for side in (0, 1):
        post.arrived((side, 1, 0, 2))
        onward(side, 2, (2, 1, 3))
    for first in (0, 3, 1):
        for side in (0, 1):
            relay(side, first)
    for step in (1, 3, 2):
        post.arrived(("codes", 2, step))
    pieces = [
        codes_all[far, near, step]
        for far in range(SIDE)
        for near in range(SIDE)
        for step in range(ids.shape[0])
    ]
    routing(me, pieces, pos, val, table, most)
    for first in (0, 3, 1):
        for side in (0, 1):
            for step in (1, 3):
                post.arrived((side, 2, first, "far", step))
    for side in (0, 1):
        for step in (1, 3, 2):
            post.arrived((side, 2, 2, step))
    post.drain()
    mine.wait()


def call_share(ids, gates, placement, tokens, experts):
    vmem = pl.BlockSpec(memory_space=pltpu.VMEM)
    smem = pl.BlockSpec(memory_space=pltpu.SMEM)
    hbm = pl.BlockSpec(memory_space=pl.ANY)
    peers = SIDE * SIDE
    total = peers * tokens.shape[0]
    return pl.pallas_call(
        share,
        out_shape=(
            jax.ShapeDtypeStruct((peers,) + tokens.shape, tokens.dtype),
            jax.ShapeDtypeStruct((experts, total), I32),
            jax.ShapeDtypeStruct((experts, total), F32),
            jax.ShapeDtypeStruct((1, TABLE), I32),
            jax.ShapeDtypeStruct((1, 128), I32),
            jax.ShapeDtypeStruct((ids.shape[0], ids.shape[2]), F32),
        ),
        in_specs=[vmem, vmem, smem, vmem],
        out_specs=(hbm, vmem, vmem, vmem, vmem, vmem),
        scratch_shapes=[
            pltpu.VMEM((SIDE, SIDE) + ids.shape, ids.dtype),
            pltpu.SemaphoreType.DMA((1,)),
            pltpu.SemaphoreType.DMA((42,)),
            pltpu.SemaphoreType.DMA((42,)),
        ],
        compiler_params=pltpu.CompilerParams(collective_id=1, has_side_effects=True),
        name="share",
    )(ids, gates, placement, tokens)


def ep_peers():
    me, z, x, at = torus()
    return [{"ep": at(0, step)} for step in (1, 2, 3)] + [{"ep": at(step, 0)} for step in (1, 2, 3)]


def settle(out, acc, parts, big, fills, sums, small, sends, recvs):
    me, z, x, at = torus()
    rows, depth = parts.shape[2:]
    half, lot = depth // 2, rows // 2
    post = Post(sends, recvs)
    axis_one = (x, z)
    axis_two = (z, x)

    def wide(side, step, part):
        to = lax.rem(axis_one[side] + step, SIDE)
        spot = (slice(None), to) if side == 0 else (to, slice(None))
        return parts.at[spot + (pl.ds(part * lot, lot), pl.ds(side * half, half))]

    def target(side, stage, step):
        along_x = (side == 0) == (stage == 1)
        return {"ep": at(0, step) if along_x else at(step, 0)}

    def flip(far, pair):
        lane = pl.multiple_of((far * 2 + pair) * 2 * rows, 2 * rows)
        turned = acc[:, pl.ds(lane, 2 * rows)].T.astype(BF16)
        for near in (0, 1):
            parts[far, pair * 2 + near] = turned[near * rows : (near + 1) * rows]

    for side in (0, 1):
        if acc is not None:
            pair = lax.div(lax.rem(x + (2 if side == 0 else 0), SIDE), 2)
            for far in range(SIDE):
                flip(far, pair)
        post.send((side, 0), wide(side, 2, LOW), big.at[side, 0], target(side, 1, 1))
        post.send((side, 1), wide(side, 2, HIGH), big.at[side, 1], target(side, 1, 3))
    for side in (0, 1):
        post.send((side, 3), wide(side, 1, HIGH), big.at[side, 3], target(side, 1, 1))
        post.send((side, 2), wide(side, 3, LOW), big.at[side, 2], target(side, 1, 3))
    for side in (0, 1):
        for part, step in ((LOW, 1), (HIGH, 3)):
            post.arrived((side, part))
            fills[side, part] = wide(side, step, part)[...] + big[side, part]
            post.send((side, 4 + part), fills.at[side, part], big.at[side, 4 + part], target(side, 1, step))
    for side in (0, 1):
        for part in (HIGH, LOW):
            post.arrived((side, 2 + part))
            post.arrived((side, 4 + part))
            sums[side, :, pl.ds(part * lot, lot), :] = (
                wide(side, 0, part)[...].astype(F32)
                + big[side, 2 + part].astype(F32)
                + big[side, 4 + part].astype(F32)
            ).astype(BF16)
        for step in (2, 1, 3):
            to = lax.rem(axis_two[side] + step, SIDE)
            post.send((side, "two", step), sums.at[side, to], small.at[side, step - 1], target(side, 2, step))
    for side in (0, 1):
        for step in (1, 3, 2):
            post.arrived((side, "two", step))
        out[:, pl.ds(side * half, half)] = (
            sums[side, axis_two[side]].astype(F32)
            + small[side, 0].astype(F32)
            + small[side, 1].astype(F32)
            + small[side, 2].astype(F32)
        )
    post.drain()


def settle_scratch(rows, depth):
    lot, half = rows // 2, depth // 2
    return [
        pltpu.VMEM((SIDE, SIDE, rows, depth), BF16),
        pltpu.VMEM((2, 6, SIDE, lot, half), BF16),
        pltpu.VMEM((2, 2, SIDE, lot, half), BF16),
        pltpu.VMEM((2, SIDE, rows, half), BF16),
        pltpu.VMEM((2, 3, rows, half), BF16),
        pltpu.SemaphoreType.DMA((18,)),
        pltpu.SemaphoreType.DMA((18,)),
    ]


def settle_alone(parts, out, *scratch):
    greet(ep_peers())
    settle(out, None, parts, *scratch)


def call_settle(parts):
    rows, depth = parts.shape[2:]
    vmem = pl.BlockSpec(memory_space=pltpu.VMEM)
    return pl.pallas_call(
        settle_alone,
        out_shape=jax.ShapeDtypeStruct((rows, depth), F32),
        in_specs=[vmem],
        out_specs=vmem,
        scratch_shapes=settle_scratch(rows, depth)[1:],
        compiler_params=pltpu.CompilerParams(collective_id=2, has_side_effects=True),
        name="settle",
    )(parts)


WAVE = 256
DEPTH = 7
ORDER = (5, 4, 3, 2, 1, 0, 6)
KINDS = (("swap", 0), ("cross", 4), ("cross", 2)) + tuple(
    (name, step)
    for name in ("far", "direct", "summed", "round", "relay", "cross")
    for step in (1, 3)
)


def core(
    waves,
    table,
    pos,
    val,
    tokens,
    gate_up,
    down,
    out,
    wide,
    narrow,
    flipped,
    wsems,
    hot,
    plain,
    picked,
    parts,
    other,
    far,
    direct,
    summed,
    fill,
    hidden,
    turned,
    acc,
    sends,
    recvs,
    *rest,
):
    me = lax.axis_index("fsdp")
    y, core_at = lax.div(me, 2), lax.rem(me, 2)
    experts, units = down.shape[0], down.shape[2]
    rows = WAVE // 8
    side = WAVE // 2
    tiles = WAVE // TILE
    partner = {"fsdp": y * 2 + 1 - core_at}
    sides = {step: {"fsdp": lax.rem(y + step, SIDE) * 2 + core_at} for step in (1, 3)}
    loads = []
    for e in range(experts):
        loads.append(pltpu.make_async_copy(gate_up.at[e], wide.at[e], wsems.at[e]))
    for e in range(experts):
        loads.append(pltpu.make_async_copy(down.at[e], narrow.at[e], wsems.at[experts + e]))
    for load in loads:
        load.start()
    greet([partner, sides[1], sides[3]] + (ep_peers() if rest else []))
    columns = (pl.ds(0, units), pl.ds(units, units))

    def half(which):
        return pl.ds(pl.multiple_of(which * side, side), side)

    def block(step):
        at = core_at * side + lax.rem(y + step, SIDE) * rows
        return pl.ds(pl.multiple_of(at, rows), rows)

    def mine(w, step, piece):
        return parts.at[w, block(step), columns[piece]]

    def route_of(kind, w):
        name, step = kind
        piece = LOW if (step == 1) == (name != "direct") else HIGH
        if name == "swap":
            return parts.at[w, half(1 - core_at)], other.at[w], partner
        if name == "far":
            return mine(w, 2, piece), far.at[w, piece], sides[step]
        if name == "direct":
            return mine(w, step, piece), direct.at[w, piece], sides[step]
        if name == "summed":
            return fill.at[w, piece], summed.at[w, piece], sides[step]
        if name == "round":
            own = hidden.at[w, block(0)]
            return own, own, sides[step]
        if name == "cross":
            whole = hidden.at[w, block(4 - step)]
            return whole, whole, partner
        at = core_at * side + lax.rem(y + 4 - step, SIDE) * rows + (step // 2) * (rows // 2)
        part = hidden.at[w, pl.ds(pl.multiple_of(at, rows // 2), rows // 2)]
        return part, part, sides[step]

    def copy(name, step, w):
        src, dst, to = route_of((name, step), w)
        k = KINDS.index((name, step))
        return pltpu.make_async_remote_copy(
            src_ref=src,
            dst_ref=dst,
            send_sem=sends.at[w, k],
            recv_sem=recvs.at[w, k],
            device_id=to,
            device_id_type=MESH,
        )

    slot = lax.broadcasted_iota(I32, (TILE, pos.shape[1]), 0)

    def produce(w):
        spot = lax.rem(w, DEPTH)

        def mark(j, _):
            e = table[w * tiles + j]
            at = pl.multiple_of(j * TILE, TILE)
            same = pos[pl.ds(e, 1), :] - (w * WAVE + at) == slot
            plain[pl.ds(at, TILE), :] = jnp.where(same, 1.0, 0.0).astype(BF16)
            hot[spot, pl.ds(at, TILE), :] = jnp.where(same, val[pl.ds(e, 1), :], 0.0).astype(BF16)
            return 0

        lax.fori_loop(0, tiles, mark, 0)
        picked[...] = jnp.dot(plain[...], tokens[...], preferred_element_type=F32).astype(BF16)

        @pl.when(w == 0)
        def _():
            for load in loads[:experts]:
                load.wait()

        def tile(which, j, _):
            j = which * (tiles // 2) + j
            e = table[w * tiles + j]
            at = pl.ds(pl.multiple_of(j * TILE, TILE), TILE)
            parts[w, at, :] = jnp.dot(
                picked[at, :], wide[e], preferred_element_type=F32
            ).astype(BF16)
            return 0

        lax.fori_loop(0, tiles // 2, functools.partial(tile, 1 - core_at), 0, unroll=True)
        copy("swap", 0, w).start()
        lax.fori_loop(0, tiles // 2, functools.partial(tile, core_at), 0, unroll=True)

    def fold(w, step):
        at = pl.ds(pl.multiple_of(lax.rem(y + step, SIDE) * rows, rows), rows)
        parts[w, block(step), :] = parts[w, block(step), :] + other[w, at, :]

    def first(w):
        copy("swap", 0, w).wait_recv()
        fold(w, 2)
        copy("far", 1, w).start()
        copy("far", 3, w).start()
        fold(w, 1)
        copy("direct", 1, w).start()
        fold(w, 3)
        copy("direct", 3, w).start()
        fold(w, 0)

    def second(w):
        for piece, step in ((LOW, 1), (HIGH, 3)):
            copy("far", step, w).wait_recv()
            fill[w, piece] = mine(w, step, piece)[...] + far[w, piece]
            copy("summed", step, w).start()

    def third(w):
        both = []
        for piece, step in ((LOW, 1), (HIGH, 3)):
            copy("direct", 4 - step, w).wait_recv()
            copy("summed", step, w).wait_recv()
            both.append(
                mine(w, 0, piece)[...].astype(F32)
                + direct[w, piece].astype(F32)
                + summed[w, piece].astype(F32)
            )
        gate, up = both
        hidden[w, block(0), :] = (gate / (1 + jnp.exp(-gate)) * up).astype(BF16)
        copy("round", 1, w).start()
        copy("round", 3, w).start()
        copy("cross", 4, w).start()

    def fourth(w):
        for step in (1, 3):
            copy("round", step, w).wait_recv()
            copy("relay", step, w).start()
            copy("cross", step, w).start()

    def fifth(w):
        for step in (1, 3):
            copy("relay", step, w).wait_recv()
        copy("cross", 2, w).start()

    def consume(w):
        spot = lax.rem(w, DEPTH)
        for step in (4, 1, 3, 2):
            copy("cross", step, w).wait_recv()

        def tile(j, _):
            e = table[w * tiles + j]
            at = pl.ds(pl.multiple_of(j * TILE, TILE), TILE)
            turned[at, :] = jnp.dot(hidden[w, at, :], flipped[e], preferred_element_type=F32)
            return 0

        lax.fori_loop(0, tiles, tile, 0, unroll=True)
        flat = turned[...].T.astype(BF16)
        for c in range(pos.shape[1] // LANES):
            lane = pl.ds(c * LANES, LANES)
            acc[:, lane] += jnp.dot(flat, hot[spot, :, lane], preferred_element_type=F32)

    acc[...] = jnp.zeros_like(acc)
    stages = (produce, first, second, third, fourth, fifth, consume)

    def turn(t, _):
        for late in ORDER:
            w = t - late

            @pl.when((w >= 0) & (w < waves))
            def _(late=late, w=w):
                stages[late](w)

        @pl.when(t == 0)
        def _():
            for load in loads[experts:]:
                load.wait()

        @pl.when(t < 4)
        def _():
            for e in (2 * t, 2 * t + 1):
                flipped[e] = narrow[e].astype(F32).T.astype(BF16)

        return 0

    lax.fori_loop(0, waves + len(stages) - 1, turn, 0)

    def drain(w, _):
        for name, step in KINDS:
            copy(name, step, w).wait_send()
        return 0

    if rest:
        settle(out, acc, *rest)
        lax.fori_loop(0, waves, drain, 0)
        return

    def flip(c, _):
        lane = pl.multiple_of(c * 256, 256)
        out[pl.ds(lane, 256), :] = acc[:, pl.ds(lane, 256)].T.astype(out.dtype)
        return 0

    lax.fori_loop(0, out.shape[0] // 256, flip, 0)
    lax.fori_loop(0, waves, drain, 0)


def call_core(waves, fused, table, pos, val, tokens, gate_up, down):
    experts, depth, width = gate_up.shape
    rows, units = WAVE // 8, width // 2
    total = tokens.shape[0]
    smem = pl.BlockSpec(memory_space=pltpu.SMEM)
    vmem = pl.BlockSpec(memory_space=pltpu.VMEM)
    hbm = pl.BlockSpec(memory_space=pl.ANY)
    piece = pltpu.VMEM((waves, 2, rows, units), BF16)
    return pl.pallas_call(
        functools.partial(core, waves),
        out_shape=jax.ShapeDtypeStruct(
            (total // (SIDE * SIDE), depth) if fused else (total, depth), F32 if fused else BF16
        ),
        in_specs=[smem, vmem, vmem, vmem, hbm, hbm],
        out_specs=vmem,
        scratch_shapes=[
            pltpu.VMEM(gate_up.shape, BF16),
            pltpu.VMEM(down.shape, BF16),
            pltpu.VMEM((experts, units, depth), BF16),
            pltpu.SemaphoreType.DMA((2 * experts,)),
            pltpu.VMEM((DEPTH, WAVE, total), BF16),
            pltpu.VMEM((WAVE, total), BF16),
            pltpu.VMEM((WAVE, depth), BF16),
            pltpu.VMEM((waves, WAVE, width), BF16),
            pltpu.VMEM((waves, WAVE // 2, width), BF16),
            piece,
            piece,
            piece,
            piece,
            pltpu.VMEM((waves, WAVE, units), BF16),
            pltpu.VMEM((WAVE, depth), F32),
            pltpu.VMEM((depth, total), F32),
            pltpu.SemaphoreType.DMA((waves, len(KINDS))),
            pltpu.SemaphoreType.DMA((waves, len(KINDS))),
        ]
        + (settle_scratch(total // (SIDE * SIDE), depth) if fused else []),
        compiler_params=pltpu.CompilerParams(
            collective_id=waves + (0 if fused else 16), has_side_effects=True, vmem_limit_bytes=62 << 20
        ),
        name="core%d" % waves + ("s" if fused else ""),
    )(table, pos, val, tokens, gate_up, down)


def local(tokens, gate_up_weight, down_weight, placement, copy_ids, gate_codes):
    steps, rows, depth = tokens.shape
    experts = gate_up_weight.shape[0]
    peers = lax.axis_size("ep")
    everyone, pos, val, table, most, totals = call_share(
        copy_ids.transpose(0, 2, 1),
        gate_codes.transpose(0, 2, 1),
        placement,
        tokens.reshape(steps * rows, depth),
        experts,
    )
    everyone = everyone.reshape(peers * steps * rows, depth)
    most = most[0, 0]
    table = table.reshape(-1)
    tiles = CHOICES[-1] * WAVE // TILE

    span = CHOICES[-1] * WAVE

    def usual(waves, *operands):
        return call_core(waves, True, operands[0][:tiles], *operands[1:])

    def beyond(table, pos, *operands):
        def chunk(at):
            part = lax.dynamic_slice(table, (at * tiles,), (tiles,))
            return call_core(CHOICES[-1], False, part, pos - at * span, *operands)

        _, sums = lax.while_loop(
            lambda c: c[0] * span < most,
            lambda c: (c[0] + 1, (c[1].astype(F32) + chunk(c[0]).astype(F32)).astype(BF16)),
            (jnp.int32(0), jnp.zeros((peers * steps * rows, depth), BF16)),
        )
        return call_settle(sums.reshape(SIDE, SIDE, steps * rows, depth))

    branches = [functools.partial(usual, waves) for waves in CHOICES] + [beyond]
    pick = jnp.int32(0)
    for waves in CHOICES:
        pick += (most > waves * WAVE).astype(I32)
    mixed = lax.switch(pick, branches, table, pos, val, everyone, gate_up_weight, down_weight)
    return (mixed.reshape(steps, rows, depth) / totals[:, :, None]).astype(BF16)


def solution(mesh):
    in_specs = (
        P(None, "ep", "fsdp"),
        P("ep", "fsdp", None),
        P("ep", "fsdp", None),
        P(),
        P(None, "ep", None),
        P(None, "ep", None),
    )
    out_specs = P(None, "ep", "fsdp")
    return jax.shard_map(local, mesh=mesh, in_specs=in_specs, out_specs=out_specs, check_vma=False)
```
